32 devices in a mesh: req: 4 (over z), seq: 8 (over y, x, core).
Axes of the slice: x: 2, y: 2, z: 4, core: 2. Of those that a mesh axis runs over, the one named last changes fastest.
Arguments:
- tokens: bfloat16 [32, 4, 2560], P('req'), may hold values from -6 to 6
- slot_of: int32 [32], replicated, may hold values from 0 to 31, each once
- cache_len: int32 [32], P('req'), may hold values from 1 to 4096, 32768 in all
- owner_shard: int32 [32, 4], P('req'), may hold values from 0 to 7
- cache_keys: bfloat16 [32, 4096, 1024], P('req', 'seq'), may hold values from -40 to 40
- stored_values: bfloat16 [32, 4096, 1024], P('req', 'seq'), may hold values from -6 to 6
- attn_gain: float32 [2560], replicated, may hold values from 0.5 to 1.5
- w_query: bfloat16 [2560, 4096], P(None, 'seq'), may hold values from -0.125 to 0.125
- key_matrix: bfloat16 [2560, 1024], P(None, 'seq'), may hold values from -0.125 to 0.125
- value_matrix: bfloat16 [2560, 1024], P(None, 'seq'), may hold values from -0.125 to 0.125
- query_gain: float32 [128], replicated, may hold values from 0.5 to 40
- key_norm_weight: float32 [128], replicated, may hold values from 0.5 to 8
- w_out: bfloat16 [4096, 2560], P('seq'), may hold values from -0.09375 to 0.09375
- mlp_gain: float32 [2560], replicated, may hold values from 0.5 to 1.5
- w_gate: bfloat16 [2560, 9728], P(None, ('req', 'seq')), may hold values from -0.125 to 0.125
- w_up: bfloat16 [2560, 9728], P(None, ('req', 'seq')), may hold values from -0.125 to 0.125
- w_down: bfloat16 [9728, 2560], P(('req', 'seq')), may hold values from -0.0625 to 0.0625
Outputs:
- outputs: bfloat16 [32, 4, 2560], P('req')
- appended: bfloat16 [32, 8, 4, 2048], P('req', 'seq')
The draws below stay inside these ranges and needn't reach their ends.
Inputs may be any that keep to these rules, and one draw needn't show every extreme that they name: `slot_of`: each slot appears once. `cache_len`: one slot has exactly 4096 cached positions; the lengths sum to 32768.
All inputs are finite; a program needn't handle non-finite values. No bound on the sum of `cache_len` on one device may be relied on, other than what follows from the above.
Results may differ from the reference program's by a relative error of at most 0.012.
The reference program's roundings to bfloat16 on the way count: a program that leaves them out, or rounds other values in their place, can miss the bound.
Values may be sent and summed in bfloat16 or wider, within the bound.
A program may use at most 128 MiB of HBM per device.

```python
import math
import jax
import jax.numpy as jnp
import numpy as np
from jax import lax

MODEL_WIDTH = 2560
QUERY_HEAD_COUNT = 32
KEY_HEADS = 8
HEAD_SIZE = 128
FF = 9728
SHARD_POSITIONS = 512
DECODE_STEPS = 4
REQUEST_TOTAL = 32
REQUEST_POSITIONS = 4096
SHARDS = 8
N_SEQ = 8


def draw_cache_keys(key, part):
    complete_shape = (REQUEST_TOTAL, REQUEST_POSITIONS, KEY_HEADS * HEAD_SIZE)
    base_draw = jnp.clip(2.0 * jax.random.normal(key, complete_shape, jnp.float32), -12.0, 12.0)
    return base_draw.astype(jnp.bfloat16)


def draw_query_gain(key, part):
    channel_ids = jnp.arange(HEAD_SIZE, dtype=jnp.int32)
    chosen = (channel_ids == HEAD_SIZE // 2 - 1) | (channel_ids == HEAD_SIZE - 1)
    base_draw = jnp.exp(jax.random.uniform(key, (HEAD_SIZE,), jnp.float32, math.log(0.5), math.log(2.0)))
    return jnp.where(chosen, 40.0, base_draw).astype(jnp.float32)


def draw_key_norm_weight(key, part):
    own_key = jax.random.fold_in(key, 7)
    channel_ids = jnp.arange(HEAD_SIZE, dtype=jnp.int32)
    chosen = (channel_ids == HEAD_SIZE // 2 - 1) | (channel_ids == HEAD_SIZE - 1)
    base_draw = jnp.exp(jax.random.uniform(own_key, (HEAD_SIZE,), jnp.float32, math.log(0.5), math.log(2.0)))
    return jnp.where(chosen, 8.0, base_draw).astype(jnp.float32)


def place_ends(array, key, low, high):
    extent = array.shape
    index_at = [jax.random.randint(jax.random.fold_in(key, axis), (), 0, extent[axis]) for axis in range(len(extent))]
    array = array.at[tuple(index_at)].set(low)
    longest = extent.index(max(extent))
    index_at[longest] = (index_at[longest] + 1) % extent[longest]
    return array.at[tuple(index_at)].set(high)


def level_of(stream_key, shape, shards, least, largest):
    factor_of, own = 1.0, jax.random.fold_in(stream_key, 6)
    for position, parts in shards:
        heights = jnp.exp(jax.random.uniform(jax.random.fold_in(own, position), (parts,), jnp.float32, least / len(shards), largest / len(shards)))
        factor_of = factor_of * jnp.repeat(heights, shape[position] // parts).reshape([-1 if axis == position else 1 for axis in range(len(shape))])
    return factor_of


def length_profile(number_of, total, limit, skew):
    loads = [(1 << 20) // math.isqrt(rank ** skew) + 1 for rank in range(2, number_of + 1)]
    spare, holding = total - limit - (number_of - 1), [1] * (number_of - 1)
    while spare > 0:
        free = [i for i in range(number_of - 1) if holding[i] < limit]
        pool, left = sum([loads[i] for i in free]), spare
        for i in free:
            extra = min(limit - holding[i], max(1, left * loads[i] // pool), spare)
            holding[i] = holding[i] + extra
            spare = spare - extra
    return np.array([limit] + holding)


def uneven_parts(key, amount, total, bound, skew):
    if amount == 2:
        one = jax.random.randint(key, (), max(1, total - bound), min(bound, total - 1) + 1)
        return jnp.stack([one, total - one])
    sizes = jnp.asarray(length_profile(amount, total, bound, skew), jnp.int32)
    twos = (amount - 1) // 2
    donor, sink = sizes[1:1 + 2 * twos:2], sizes[2:2 + 2 * twos:2]
    slack = jnp.minimum(donor - 1, bound - sink)
    passed = jax.random.randint(jax.random.fold_in(key, 1), (twos,), 0, 1 << 20) % (slack + 1)
    sizes = sizes.at[1:1 + 2 * twos:2].set(donor - passed).at[2:2 + 2 * twos:2].set(sink + passed)
    return sizes[jax.random.permutation(jax.random.fold_in(key, 2), amount)]


def normal_values(stream_key, shape, spread, bound, cuts=(), kind=jnp.bfloat16):
    values = jax.random.normal(stream_key, shape, jnp.float32) * spread
    if len(cuts) > 0:
        values = level_of(stream_key, shape, cuts, -0.22, 0.18) * values
    return jnp.clip(values, min=-bound, max=bound).astype(kind)


def setup_inputs(seed: int = 0) -> dict:
    arg_keys = jax.random.split(jax.random.key(seed), 18)
    tokens = normal_values(arg_keys[0], (REQUEST_TOTAL, DECODE_STEPS, MODEL_WIDTH), 1.0, 6.0, ((0, 4),))
    slot_of = jax.random.permutation(arg_keys[1], REQUEST_TOTAL).astype(jnp.int32)
    cache_len = uneven_parts(arg_keys[2], REQUEST_TOTAL, REQUEST_TOTAL * REQUEST_POSITIONS // 4, REQUEST_POSITIONS, 2).astype(jnp.int32)
    owner_shard = place_ends(jax.random.randint(arg_keys[3], (REQUEST_TOTAL, DECODE_STEPS), 0, SHARDS), jax.random.fold_in(arg_keys[3], 1), 0, SHARDS - 1).astype(jnp.int32)
    cache_keys = draw_cache_keys(jax.random.fold_in(arg_keys[17], 71), 0)
    stored_values = normal_values(arg_keys[5], (REQUEST_TOTAL, REQUEST_POSITIONS, KEY_HEADS * HEAD_SIZE), 1.0, 6.0, ((0, 4), (1, 8)))
    attn_gain = jnp.clip(1.0 + 0.1 * jax.random.normal(arg_keys[6], (MODEL_WIDTH,), jnp.float32), 0.5, 1.5)
    w_query = normal_values(arg_keys[7], (MODEL_WIDTH, QUERY_HEAD_COUNT * HEAD_SIZE), MODEL_WIDTH ** -0.5, 0.125, ((1, 8),))
    key_matrix = normal_values(arg_keys[8], (MODEL_WIDTH, KEY_HEADS * HEAD_SIZE), MODEL_WIDTH ** -0.5, 0.125, ((1, 8),))
    value_matrix = normal_values(arg_keys[9], (MODEL_WIDTH, KEY_HEADS * HEAD_SIZE), MODEL_WIDTH ** -0.5, 0.125, ((1, 8),))
    query_gain = draw_query_gain(jax.random.fold_in(arg_keys[17], 71), 0)
    key_norm_weight = draw_key_norm_weight(jax.random.fold_in(arg_keys[17], 71), 0)
    w_out = normal_values(arg_keys[12], (QUERY_HEAD_COUNT * HEAD_SIZE, MODEL_WIDTH), (QUERY_HEAD_COUNT * HEAD_SIZE) ** -0.5, 0.09375, ((0, 8),))
    mlp_gain = jnp.clip(1.0 + 0.1 * jax.random.normal(arg_keys[13], (MODEL_WIDTH,), jnp.float32), 0.5, 1.5)
    w_gate = normal_values(arg_keys[14], (MODEL_WIDTH, FF), MODEL_WIDTH ** -0.5, 0.125, ((1, 32),))
    w_up = normal_values(arg_keys[15], (MODEL_WIDTH, FF), MODEL_WIDTH ** -0.5, 0.125, ((1, 32),))
    w_down = normal_values(arg_keys[16], (FF, MODEL_WIDTH), FF ** -0.5, 0.0625, ((0, 32),))
    return {"tokens": tokens, "slot_of": slot_of, "cache_len": cache_len, "owner_shard": owner_shard, "cache_keys": cache_keys, "stored_values": stored_values, "attn_gain": attn_gain, "w_query": w_query, "key_matrix": key_matrix, "value_matrix": value_matrix, "query_gain": query_gain, "key_norm_weight": key_norm_weight, "w_out": w_out, "mlp_gain": mlp_gain, "w_gate": w_gate, "w_up": w_up, "w_down": w_down}


EPSILON = 1e-06
ROPE_BASE = 1000000.0
MASKED = -1e+30

def root_mean_scale(tensor, gain_vec):
    mean_square = lax.optimization_barrier(jnp.mean(tensor * tensor, axis=-1, keepdims=True))
    return tensor * lax.rsqrt(mean_square + EPSILON) * gain_vec

def apply_rotary(tensor, positions):
    half_dim = tensor.shape[-1] // 2
    frequency = ROPE_BASE ** (-2.0 * jnp.arange(half_dim, dtype=jnp.float32) / tensor.shape[-1])
    angles = positions[..., None] * frequency
    cosine = jnp.cos(angles)
    sine_part = jnp.sin(angles)
    front_half = tensor[..., :half_dim]
    back_half = tensor[..., half_dim:]
    return jnp.concatenate([front_half * cosine - back_half * sine_part, back_half * cosine + front_half * sine_part], axis=-1)

def attend_one(query_rows, position_keys, position_values, length, incoming_keys, incoming_values, owner_row, decode_index):
    score_scale = 1.0 / math.sqrt(HEAD_SIZE)
    key_layout = position_keys.astype(jnp.float32).reshape(N_SEQ, SHARD_POSITIONS, KEY_HEADS, HEAD_SIZE)
    value_layout = position_values.astype(jnp.float32).reshape(N_SEQ, SHARD_POSITIONS, KEY_HEADS, HEAD_SIZE)
    query_groups = query_rows.astype(jnp.float32).reshape(KEY_HEADS, QUERY_HEAD_COUNT // KEY_HEADS, HEAD_SIZE)
    scores = jnp.einsum('kgd,bpkd->kgbp', query_groups, key_layout) * score_scale
    in_cache = (jnp.arange(N_SEQ * SHARD_POSITIONS, dtype=jnp.int32) < length).reshape(N_SEQ, SHARD_POSITIONS)
    scores = jnp.where(in_cache[None, None], scores, MASKED)
    fresh_scores = jnp.einsum('kgd,skd->kgs', query_groups, incoming_keys.astype(jnp.float32)) * score_scale
    slot_live = jnp.arange(DECODE_STEPS, dtype=jnp.int32) <= decode_index
    owns = (owner_row[:, None] == jnp.arange(N_SEQ, dtype=jnp.int32)[None, :]) & slot_live[:, None]
    fresh_blocks = jnp.where(owns[None, None], fresh_scores[..., None], MASKED)
    block_max = jnp.maximum(lax.optimization_barrier(jnp.max(scores, axis=-1)), lax.optimization_barrier(jnp.max(fresh_blocks, axis=2)))
    weights = jnp.where(in_cache[None, None], jnp.exp(scores - block_max[..., None]), 0.0)
    fresh_weights = jnp.where(owns[None, None], jnp.exp(fresh_blocks - block_max[:, :, None, :]), 0.0)
    block_sum = lax.optimization_barrier(jnp.sum(weights, axis=-1)) + lax.optimization_barrier(jnp.sum(fresh_weights, axis=2))
    rounded = lax.optimization_barrier(weights.astype(jnp.bfloat16)).astype(jnp.float32)
    fresh_rounded = lax.optimization_barrier(fresh_weights.astype(jnp.bfloat16)).astype(jnp.float32)
    block_out = jnp.einsum('kgbp,bpkd->kgbd', rounded, value_layout)
    block_out = block_out + jnp.einsum('kgsb,skd->kgbd', fresh_rounded, incoming_values.astype(jnp.float32))
    joint = lax.optimization_barrier(jnp.max(block_max, axis=-1))
    factor = jnp.exp(block_max - joint[..., None])
    result = lax.optimization_barrier(jnp.sum(factor[..., None] * block_out, axis=2)) / lax.optimization_barrier(jnp.sum(factor * block_sum, axis=2))[..., None]
    return result.reshape(QUERY_HEAD_COUNT, HEAD_SIZE).astype(jnp.bfloat16)

def reference(tokens, slot_of, cache_len, owner_shard, cache_keys, stored_values, attn_gain, w_query, key_matrix, value_matrix, query_gain, key_norm_weight, w_out, mlp_gain, w_gate, w_up, w_down):
    overall_rows = tokens.shape[0]
    selector = (slot_of[None, :] == jnp.arange(overall_rows, dtype=jnp.int32)[:, None]).astype(jnp.float32)
    inputs = jnp.einsum('ji,isd->jsd', selector, tokens.astype(jnp.float32), precision=lax.Precision.HIGHEST)
    incoming_keys = jnp.zeros((overall_rows, DECODE_STEPS, KEY_HEADS, HEAD_SIZE), jnp.bfloat16)
    incoming_values = jnp.zeros((overall_rows, DECODE_STEPS, KEY_HEADS, HEAD_SIZE), jnp.bfloat16)
    results = []
    for decode_index in range(DECODE_STEPS):
        current = inputs[:, decode_index]
        normed = root_mean_scale(current, attn_gain).astype(jnp.bfloat16)
        query_raw = jnp.dot(normed, w_query, preferred_element_type=jnp.float32).astype(jnp.bfloat16)
        unnormed_keys = jnp.dot(normed, key_matrix, preferred_element_type=jnp.float32).astype(jnp.bfloat16)
        latest_value = jnp.dot(normed, value_matrix, preferred_element_type=jnp.float32).astype(jnp.bfloat16)
        decode_position = (cache_len + decode_index).astype(jnp.float32)[:, None]
        query_rows = apply_rotary(root_mean_scale(query_raw.astype(jnp.float32).reshape(overall_rows, QUERY_HEAD_COUNT, HEAD_SIZE), query_gain), decode_position).astype(jnp.bfloat16)
        latest_key = apply_rotary(root_mean_scale(unnormed_keys.astype(jnp.float32).reshape(overall_rows, KEY_HEADS, HEAD_SIZE), key_norm_weight), decode_position).astype(jnp.bfloat16)
        incoming_keys = incoming_keys.at[:, decode_index].set(latest_key)
        incoming_values = incoming_values.at[:, decode_index].set(latest_value.reshape(overall_rows, KEY_HEADS, HEAD_SIZE))

        def per_request(packed):
            return attend_one(packed[0], packed[1], packed[2], packed[3], packed[4], packed[5], packed[6], decode_index)
        attended = lax.map(per_request, (query_rows, cache_keys, stored_values, cache_len, incoming_keys, incoming_values, owner_shard))
        attended = attended.reshape(overall_rows, QUERY_HEAD_COUNT * HEAD_SIZE)
        residual = current + jnp.dot(attended, w_out, preferred_element_type=jnp.float32)
        mlp_in = root_mean_scale(residual, mlp_gain).astype(jnp.bfloat16)
        gate_part = jnp.dot(mlp_in, w_gate, preferred_element_type=jnp.float32)
        up_part = jnp.dot(mlp_in, w_up, preferred_element_type=jnp.float32)
        hidden = (jax.nn.silu(gate_part) * up_part).astype(jnp.bfloat16)
        results.append((residual + jnp.dot(hidden, w_down, preferred_element_type=jnp.float32)).astype(jnp.bfloat16))
    outputs = jnp.stack(results, axis=1)
    stacked_incoming = jnp.concatenate([incoming_keys.reshape(overall_rows, DECODE_STEPS, KEY_HEADS * HEAD_SIZE), incoming_values.reshape(overall_rows, DECODE_STEPS, KEY_HEADS * HEAD_SIZE)], axis=-1)
    owns_all = owner_shard[:, None, :] == jnp.arange(N_SEQ, dtype=jnp.int32)[None, :, None]
    appended = jnp.where(owns_all[..., None], stacked_incoming[:, None], jnp.zeros((), jnp.bfloat16))
    return (outputs, appended.astype(jnp.bfloat16))
```

```python
import functools
import math

import jax
import jax.numpy as jnp
from jax import lax
from jax.experimental import pallas as pl
from jax.experimental.pallas import tpu as pltpu
from jax.sharding import PartitionSpec as P

EPSILON = 1e-06
ROPE_BASE = 1000000.0
MASKED = -1e30


def root_mean_scale(tensor, gain_vec):
    mean_square = jnp.mean(tensor * tensor, axis=-1, keepdims=True)
    return tensor * lax.rsqrt(mean_square + EPSILON) * gain_vec


def apply_rotary(tensor, positions):
    half_dim = tensor.shape[-1] // 2
    frequency = ROPE_BASE ** (-2.0 * jnp.arange(half_dim, dtype=jnp.float32) / tensor.shape[-1])
    angles = positions[..., None] * frequency
    cosine = jnp.cos(angles)
    sine_part = jnp.sin(angles)
    front_half = tensor[..., :half_dim]
    back_half = tensor[..., half_dim:]
    return jnp.concatenate(
        [front_half * cosine - back_half * sine_part, back_half * cosine + front_half * sine_part],
        axis=-1,
    )


def attention_kernel(kv_heads, query_heads, here_ref, live_ref, q_ref, k_ref, v_ref, fk_ref, fv_ref,
                     out_ref, max_ref, sum_ref):
    slot = pl.program_id(0)
    rows, head_dim = q_ref.shape[1], q_ref.shape[2]
    span = k_ref.shape[1]
    pad = fk_ref.shape[1]
    width = kv_heads * head_dim
    group = query_heads // kv_heads
    scale = 1.0 / math.sqrt(head_dim)
    own_kv = lax.rem(lax.broadcasted_iota(jnp.int32, (rows, width), 0), query_heads) // group
    lane_kv = lax.broadcasted_iota(jnp.int32, (rows, width), 1) // head_dim
    q = q_ref[0]
    wide = jnp.where(own_kv == lane_kv, jnp.concatenate([q] * kv_heads, axis=1), jnp.zeros((), q.dtype))
    nt = (((1,), (1,)), ((), ()))
    scores = lax.dot_general(wide, k_ref[0], nt, preferred_element_type=jnp.float32) * scale
    in_cache = lax.broadcasted_iota(jnp.int32, (rows, span), 1) < here_ref[slot]
    scores = jnp.where(in_cache, scores, MASKED)
    fresh = lax.dot_general(wide, fk_ref[0], nt, preferred_element_type=jnp.float32) * scale
    step_row = lax.broadcasted_iota(jnp.int32, (rows, pad), 0) // query_heads
    step_lane = lax.broadcasted_iota(jnp.int32, (rows, pad), 1)
    live = (step_lane <= step_row) & (live_ref[0, 0:1, :] > 0)
    fresh = jnp.where(live, fresh, MASKED)
    top = jnp.maximum(
        jnp.max(scores, axis=1, keepdims=True), jnp.max(fresh, axis=1, keepdims=True)
    )
    weights = jnp.where(in_cache, jnp.exp(scores - top), 0.0)
    fresh_weights = jnp.where(live, jnp.exp(fresh - top), 0.0)
    total = jnp.sum(weights, axis=1, keepdims=True) + jnp.sum(fresh_weights, axis=1, keepdims=True)
    product = jnp.dot(weights.astype(jnp.bfloat16), v_ref[0], preferred_element_type=jnp.float32)
    product = product + jnp.dot(
        fresh_weights.astype(jnp.bfloat16), fv_ref[0], preferred_element_type=jnp.float32
    )
    product = jnp.where(own_kv == lane_kv, product, 0.0)
    picked = product[:, :head_dim]
    for head in range(1, kv_heads):
        picked = picked + product[:, head * head_dim:(head + 1) * head_dim]
    out_ref[0] = picked
    max_ref[0] = jnp.broadcast_to(top, (rows, head_dim))
    sum_ref[0] = jnp.broadcast_to(total, (rows, head_dim))


def body(
    tokens,
    slot_of,
    cache_len,
    owner_shard,
    cache_keys,
    stored_values,
    attn_gain,
    w_query,
    key_matrix,
    value_matrix,
    query_gain,
    key_norm_weight,
    w_out,
    mlp_gain,
    w_gate,
    w_up,
    w_down,
):
    group_id = lax.axis_index("req")
    shard_id = lax.axis_index("seq")
    shard_count = lax.axis_size("seq")
    row_count = cache_len.shape[0]
    span_len = cache_keys.shape[1]
    step_count, model_width = tokens.shape[1:]
    head_dim = query_gain.shape[0]
    kv_heads = cache_keys.shape[2] // head_dim
    query_heads = w_query.shape[1] * shard_count // head_dim
    heads_here = query_heads // shard_count
    all_rows = row_count * step_count
    arrived = lax.all_gather(tokens, "req", axis=0, tiled=True)
    slot_ids = group_id * row_count + jnp.arange(row_count, dtype=jnp.int32)
    selector = (slot_of[None, :] == slot_ids[:, None]).astype(jnp.bfloat16)
    inputs = jnp.einsum("ji,isd->jsd", selector, arrived, preferred_element_type=jnp.float32)
    current = inputs.reshape(all_rows, model_width)
    normed = root_mean_scale(current, attn_gain).astype(jnp.bfloat16)
    parts = [
        jnp.dot(normed, matrix, preferred_element_type=jnp.float32).astype(jnp.bfloat16)
        for matrix in (w_query, key_matrix, value_matrix)
    ]
    cut = [parts[0].shape[1], parts[0].shape[1] + parts[1].shape[1]]
    gathered = lax.all_gather(jnp.concatenate(parts, axis=1), "seq", axis=0)
    gathered = jnp.transpose(gathered, (1, 0, 2))
    query_raw = gathered[:, :, :cut[0]].reshape(row_count, step_count, query_heads, head_dim)
    key_raw = gathered[:, :, cut[0]:cut[1]].reshape(row_count, step_count, kv_heads, head_dim)
    incoming_values = gathered[:, :, cut[1]:].reshape(row_count, step_count, kv_heads * head_dim)
    position = (cache_len[:, None] + jnp.arange(step_count, dtype=jnp.int32)).astype(jnp.float32)
    queries = apply_rotary(
        root_mean_scale(query_raw.astype(jnp.float32), query_gain), position[..., None]
    ).astype(jnp.bfloat16)
    incoming_keys = apply_rotary(
        root_mean_scale(key_raw.astype(jnp.float32), key_norm_weight), position[..., None]
    ).astype(jnp.bfloat16).reshape(row_count, step_count, kv_heads * head_dim)
    owned_here = owner_shard == shard_id
    pad = 128
    widen = ((0, 0), (0, pad - step_count), (0, 0))
    live = jnp.pad(owned_here.astype(jnp.int32), ((0, 0), (0, pad - step_count)))
    live = jnp.broadcast_to(live[:, None, :], (row_count, 8, pad))
    here = cache_len - shard_id * span_len
    packed_rows = step_count * query_heads
    wide_dim = kv_heads * head_dim
    slot_block = lambda *shape: pl.BlockSpec((1,) + shape, lambda i, *_: (i,) + (0,) * len(shape))
    out_type = jax.ShapeDtypeStruct((row_count, packed_rows, head_dim), jnp.float32)
    block_out, block_max, block_sum = pl.pallas_call(
        functools.partial(attention_kernel, kv_heads, query_heads),
        out_shape=(out_type,) * 3,
        grid_spec=pltpu.PrefetchScalarGridSpec(
            num_scalar_prefetch=1,
            grid=(row_count,),
            in_specs=[
                slot_block(8, pad),
                slot_block(packed_rows, head_dim),
                slot_block(span_len, wide_dim),
                slot_block(span_len, wide_dim),
                slot_block(pad, wide_dim),
                slot_block(pad, wide_dim),
            ],
            out_specs=[slot_block(packed_rows, head_dim)] * 3,
        ),
    )(
        here,
        live,
        queries.reshape(row_count, packed_rows, head_dim),
        cache_keys,
        stored_values,
        jnp.pad(incoming_keys, widen),
        jnp.pad(incoming_values, widen),
    )
    split = lambda a: a.reshape(all_rows, shard_count, heads_here, -1)
    stats = jnp.concatenate([split(block_max)[..., :1], split(block_sum)[..., :1]], axis=-1)
    payload = jnp.concatenate(
        [
            split(block_out).reshape(all_rows, shard_count, -1),
            stats.reshape(all_rows, shard_count, -1),
        ],
        axis=-1,
    )
    traded = lax.all_to_all(payload, "seq", split_axis=1, concat_axis=0, tiled=False)
    wide_out = heads_here * head_dim
    outs = traded[..., :wide_out].reshape(shard_count, all_rows, heads_here, head_dim)
    stats = traded[..., wide_out:].reshape(shard_count, all_rows, heads_here, 2)
    top = jnp.max(stats[..., 0], axis=0)
    factor = jnp.exp(stats[..., 0] - top)
    numer = jnp.sum(factor[..., None] * outs, axis=0)
    denom = jnp.sum(factor * stats[..., 1], axis=0)
    attended = (numer / denom[..., None]).astype(jnp.bfloat16).reshape(all_rows, wide_out)
    projected = lax.psum_scatter(
        jnp.dot(attended, w_out, preferred_element_type=jnp.float32),
        "seq",
        scatter_dimension=0,
        tiled=True,
    )
    rows_here = all_rows // shard_count
    residual = projected + lax.dynamic_slice_in_dim(current, shard_id * rows_here, rows_here, 0)
    mlp_in = root_mean_scale(residual, mlp_gain).astype(jnp.bfloat16)
    piece = lax.all_gather(mlp_in, ("req", "seq"), axis=0, tiled=True)
    gate_part = jnp.dot(piece, w_gate, preferred_element_type=jnp.float32)
    up_part = jnp.dot(piece, w_up, preferred_element_type=jnp.float32)
    hidden = (jax.nn.silu(gate_part) * up_part).astype(jnp.bfloat16)
    down = lax.psum_scatter(
        jnp.dot(hidden, w_down, preferred_element_type=jnp.float32),
        ("req", "seq"),
        scatter_dimension=0,
        tiled=True,
    )
    finished = (residual + down).astype(jnp.bfloat16)
    outputs = lax.all_gather(finished, "seq", axis=0, tiled=True)
    outputs = outputs.reshape(row_count, step_count, model_width)
    stacked_incoming = jnp.concatenate([incoming_keys, incoming_values], axis=-1)
    appended = jnp.where(owned_here[..., None], stacked_incoming, jnp.zeros((), jnp.bfloat16))
    return (outputs, appended[:, None])


def solution(mesh):
    in_specs = (
        P("req", None, None),
        P(),
        P("req"),
        P("req", None),
        P("req", "seq", None),
        P("req", "seq", None),
        P(),
        P(None, "seq"),
        P(None, "seq"),
        P(None, "seq"),
        P(),
        P(),
        P("seq", None),
        P(),
        P(None, ("req", "seq")),
        P(None, ("req", "seq")),
        P(("req", "seq"), None),
    )
    out_specs = (P("req", None, None), P("req", "seq", None, None))
    return jax.shard_map(body, mesh=mesh, in_specs=in_specs, out_specs=out_specs, check_vma=False)
```

```python
import functools
import math

import jax
import jax.numpy as jnp
from jax import lax
from jax.experimental import pallas as pl
from jax.experimental.pallas import tpu as pltpu
from jax.sharding import PartitionSpec as P

EPSILON = 1e-06
ROPE_BASE = 1000000.0
MASKED = -1e30


def root_mean_scale(tensor, gain_vec):
    mean_square = jnp.mean(tensor * tensor, axis=-1, keepdims=True)
    return tensor * lax.rsqrt(mean_square + EPSILON) * gain_vec


def apply_rotary(tensor, positions):
    half_dim = tensor.shape[-1] // 2
    frequency = ROPE_BASE ** (-2.0 * jnp.arange(half_dim, dtype=jnp.float32) / tensor.shape[-1])
    angles = positions[..., None] * frequency
    cosine = jnp.cos(angles)
    sine_part = jnp.sin(angles)
    front_half = tensor[..., :half_dim]
    back_half = tensor[..., half_dim:]
    return jnp.concatenate(
        [front_half * cosine - back_half * sine_part, back_half * cosine + front_half * sine_part],
        axis=-1,
    )


def attention_kernel(kv_heads, query_heads, here_ref, live_ref, q_ref, k_ref, v_ref, fk_ref, fv_ref,
                     out_ref, max_ref, sum_ref):
    slot = pl.program_id(0)
    rows, head_dim = q_ref.shape[1], q_ref.shape[2]
    span = k_ref.shape[1]
    pad = fk_ref.shape[1]
    width = kv_heads * head_dim
    group = query_heads // kv_heads
    scale = 1.0 / math.sqrt(head_dim)
    own_kv = lax.rem(lax.broadcasted_iota(jnp.int32, (rows, width), 0), query_heads) // group
    lane_kv = lax.broadcasted_iota(jnp.int32, (rows, width), 1) // head_dim
    q = q_ref[0]
    wide = jnp.where(own_kv == lane_kv, jnp.concatenate([q] * kv_heads, axis=1), jnp.zeros((), q.dtype))
    nt = (((1,), (1,)), ((), ()))
    scores = lax.dot_general(wide, k_ref[0], nt, preferred_element_type=jnp.float32) * scale
    in_cache = lax.broadcasted_iota(jnp.int32, (rows, span), 1) < here_ref[slot]
    scores = jnp.where(in_cache, scores, MASKED)
    fresh = lax.dot_general(wide, fk_ref[0], nt, preferred_element_type=jnp.float32) * scale
    step_row = lax.broadcasted_iota(jnp.int32, (rows, pad), 0) // query_heads
    step_lane = lax.broadcasted_iota(jnp.int32, (rows, pad), 1)
    live = (step_lane <= step_row) & (live_ref[0, 0:1, :] > 0)
    fresh = jnp.where(live, fresh, MASKED)
    top = jnp.maximum(
        jnp.max(scores, axis=1, keepdims=True), jnp.max(fresh, axis=1, keepdims=True)
    )
    weights = jnp.where(in_cache, jnp.exp(scores - top), 0.0)
    fresh_weights = jnp.where(live, jnp.exp(fresh - top), 0.0)
    total = jnp.sum(weights, axis=1, keepdims=True) + jnp.sum(fresh_weights, axis=1, keepdims=True)
    product = jnp.dot(weights.astype(jnp.bfloat16), v_ref[0], preferred_element_type=jnp.float32)
    product = product + jnp.dot(
        fresh_weights.astype(jnp.bfloat16), fv_ref[0], preferred_element_type=jnp.float32
    )
    product = jnp.where(own_kv == lane_kv, product, 0.0)
    picked = product[:, :head_dim]
    for head in range(1, kv_heads):
        picked = picked + product[:, head * head_dim:(head + 1) * head_dim]
    out_ref[0] = picked
    max_ref[0] = jnp.broadcast_to(top, (rows, head_dim))
    sum_ref[0] = jnp.broadcast_to(total, (rows, head_dim))


def tail_kernel(ring, plane, steps, attended_ref, current_ref, gain_ref, w_out_hbm, gate_hbm, up_hbm,
                down_hbm, out_ref, w_out, w_gate, w_up, w_down, proj_send, proj_land, mlp_all, half_send,
                half_land, quad_send, quad_land, ring_send, ring_land, final, weight_sem, send_sem, recv_sem):
    group = lax.axis_index("req")
    shard = lax.axis_index("seq")
    chips = plane // 2
    core, chip = lax.rem(shard, 2), shard // 2
    other = 1 - core
    partner = chip * 2 + other
    order = core * chips + chip
    mesh_type = pl.DeviceIdType.MESH

    weights = [
        pltpu.make_async_copy(src, dst, weight_sem.at[i])
        for i, (src, dst) in enumerate(
            ((w_out_hbm, w_out), (gate_hbm, w_gate), (up_hbm, w_up), (down_hbm, w_down))
        )
    ]
    for copy in weights:
        copy.start()
    plane_peers = [lax.rem(shard + d, plane) for d in range(1, plane)]
    ring_peers = [lax.rem(group + d, ring) for d in range(1, ring)]
    chip_peers = [lax.rem(chip + d, chips) * 2 + core for d in range(1, chips)]
    barrier = pltpu.get_barrier_semaphore()
    for peer in plane_peers:
        pl.semaphore_signal(barrier, inc=1, device_id=(group, peer), device_id_type=mesh_type)
    for peer in ring_peers:
        pl.semaphore_signal(barrier, inc=1, device_id=(peer, shard), device_id_type=mesh_type)
    used = [0]
    sent = []

    def send(src, dst, device):
        index = used[0]
        used[0] += 1
        copy = pltpu.make_async_remote_copy(
            src_ref=src, dst_ref=dst, send_sem=send_sem.at[index], recv_sem=recv_sem.at[index],
            device_id=device, device_id_type=mesh_type,
        )
        copy.start()
        sent.append(copy)
        return copy

    weights[0].wait()
    projected = jnp.dot(attended_ref[...], w_out[...], preferred_element_type=jnp.float32)
    for target in range(plane):
        proj_send[target] = projected[target * steps:(target + 1) * steps].astype(jnp.bfloat16)
    pl.semaphore_wait(barrier, plane - 1 + ring - 1)
    copies = [
        send(proj_send.at[peer], proj_land.at[d], (group, peer))
        for d, peer in enumerate(plane_peers)
    ]
    residual = current_ref[...] + proj_send[shard].astype(jnp.float32)
    for d, copy in enumerate(copies):
        copy.wait_recv()
        residual = residual + proj_land[d].astype(jnp.float32)
    mlp_all[order, group] = root_mean_scale(residual, gain_ref[...]).astype(jnp.bfloat16)

    own = mlp_all.at[order, group]
    copies = [send(own, own, (peer, shard)) for peer in ring_peers]
    for copy in copies:
        copy.wait_recv()
    own = mlp_all.at[order]
    copies = [send(own, own, (group, peer)) for peer in chip_peers]
    across = [send(own, own, (group, partner))]
    for d, copy in enumerate(copies):
        copy.wait_recv()
        came = mlp_all.at[core * chips + lax.rem(chip + chips - (d + 1), chips)]
        across.append(send(came, came, (group, partner)))
    for copy in across:
        copy.wait_recv()

    width = mlp_all.shape[-1]
    rows = plane * ring * steps
    mlp_in = mlp_all[...].astype(jnp.float32).reshape(rows, width).astype(jnp.bfloat16)
    weights[1].wait()
    gate_part = jnp.dot(mlp_in, w_gate[...], preferred_element_type=jnp.float32)
    weights[2].wait()
    up_part = jnp.dot(mlp_in, w_up[...], preferred_element_type=jnp.float32)
    hidden = (gate_part / (1.0 + jnp.exp(-gate_part)) * up_part).astype(jnp.bfloat16)
    weights[3].wait()
    down = jnp.dot(hidden, w_down[...], preferred_element_type=jnp.float32)
    half = rows // 2
    half_send[0] = down[:half].astype(jnp.bfloat16)
    half_send[1] = down[half:].astype(jnp.bfloat16)
    copy = send(half_send.at[other], half_land, (group, partner))
    copy.wait_recv()
    both = half_send[core].astype(jnp.float32) + half_land[...].astype(jnp.float32)
    quad = ring * steps
    for target in range(chips):
        quad_send[target] = both[target * quad:(target + 1) * quad].astype(jnp.bfloat16)
    copies = [
        send(quad_send.at[peer // 2], quad_land.at[d], (group, peer))
        for d, peer in enumerate(chip_peers)
    ]
    summed = quad_send[chip].astype(jnp.float32)
    for d, copy in enumerate(copies):
        copy.wait_recv()
        summed = summed + quad_land[d].astype(jnp.float32)
    for target in range(ring):
        ring_send[target] = summed[target * steps:(target + 1) * steps].astype(jnp.bfloat16)
    copies = [
        send(ring_send.at[peer], ring_land.at[d], (peer, shard)) for d, peer in enumerate(ring_peers)
    ]
    total = residual + ring_send[group].astype(jnp.float32)
    for d, copy in enumerate(copies):
        copy.wait_recv()
        total = total + ring_land[d].astype(jnp.float32)
    final[shard] = total.astype(jnp.bfloat16)
    own = final.at[shard]
    copies = [send(own, own, (group, peer)) for peer in plane_peers]
    for copy in copies:
        copy.wait_recv()
    out_ref[...] = final[...]
    for copy in sent:
        copy.wait_send()


def run_tail(attended, current, mlp_gain, w_out, w_gate, w_up, w_down, ring, plane, steps):
    width = w_out.shape[1]
    rows = plane * ring * steps
    chips = plane // 2
    bf16 = jnp.bfloat16
    copies = 3 * (plane - 1) + 3 * (ring - 1) + 3 * chips + 4
    vmem = pl.BlockSpec(memory_space=pltpu.VMEM)
    anywhere = pl.BlockSpec(memory_space=pl.ANY)
    return pl.pallas_call(
        functools.partial(tail_kernel, ring, plane, steps),
        out_shape=jax.ShapeDtypeStruct((plane, steps, width), bf16),
        in_specs=[vmem] * 3 + [anywhere] * 4,
        out_specs=vmem,
        scratch_shapes=[
            pltpu.VMEM(w_out.shape, bf16),
            pltpu.VMEM(w_gate.shape, bf16),
            pltpu.VMEM(w_up.shape, bf16),
            pltpu.VMEM(w_down.shape, bf16),
            pltpu.VMEM((plane, steps, width), bf16),
            pltpu.VMEM((plane - 1, steps, width), bf16),
            pltpu.VMEM((plane, ring, steps, width), bf16),
            pltpu.VMEM((2, rows // 2, width), bf16),
            pltpu.VMEM((rows // 2, width), bf16),
            pltpu.VMEM((chips, ring * steps, width), bf16),
            pltpu.VMEM((chips - 1, ring * steps, width), bf16),
            pltpu.VMEM((ring, steps, width), bf16),
            pltpu.VMEM((ring - 1, steps, width), bf16),
            pltpu.VMEM((plane, steps, width), bf16),
            pltpu.SemaphoreType.DMA((4,)),
            pltpu.SemaphoreType.DMA((copies,)),
            pltpu.SemaphoreType.DMA((copies,)),
        ],
        compiler_params=pltpu.CompilerParams(collective_id=0, has_side_effects=True),
    )(attended, current, mlp_gain, w_out, w_gate, w_up, w_down)


def body(
    tokens,
    slot_of,
    cache_len,
    owner_shard,
    cache_keys,
    stored_values,
    attn_gain,
    w_query,
    key_matrix,
    value_matrix,
    query_gain,
    key_norm_weight,
    w_out,
    mlp_gain,
    w_gate,
    w_up,
    w_down,
):
    group_id = lax.axis_index("req")
    shard_id = lax.axis_index("seq")
    shard_count = lax.axis_size("seq")
    row_count = cache_len.shape[0]
    span_len = cache_keys.shape[1]
    step_count, model_width = tokens.shape[1:]
    head_dim = query_gain.shape[0]
    kv_heads = cache_keys.shape[2] // head_dim
    query_heads = w_query.shape[1] * shard_count // head_dim
    heads_here = query_heads // shard_count
    all_rows = row_count * step_count
    arrived = lax.all_gather(tokens, "req", axis=0, tiled=True)
    slot_ids = group_id * row_count + jnp.arange(row_count, dtype=jnp.int32)
    selector = (slot_of[None, :] == slot_ids[:, None]).astype(jnp.bfloat16)
    inputs = jnp.einsum("ji,isd->jsd", selector, arrived, preferred_element_type=jnp.float32)
    current = inputs.reshape(all_rows, model_width)
    normed = root_mean_scale(current, attn_gain).astype(jnp.bfloat16)
    parts = [
        jnp.dot(normed, matrix, preferred_element_type=jnp.float32).astype(jnp.bfloat16)
        for matrix in (w_query, key_matrix, value_matrix)
    ]
    cut = [parts[0].shape[1], parts[0].shape[1] + parts[1].shape[1]]
    gathered = lax.all_gather(jnp.concatenate(parts, axis=1), "seq", axis=0)
    gathered = jnp.transpose(gathered, (1, 0, 2))
    query_raw = gathered[:, :, :cut[0]].reshape(row_count, step_count, query_heads, head_dim)
    key_raw = gathered[:, :, cut[0]:cut[1]].reshape(row_count, step_count, kv_heads, head_dim)
    incoming_values = gathered[:, :, cut[1]:].reshape(row_count, step_count, kv_heads * head_dim)
    position = (cache_len[:, None] + jnp.arange(step_count, dtype=jnp.int32)).astype(jnp.float32)
    queries = apply_rotary(
        root_mean_scale(query_raw.astype(jnp.float32), query_gain), position[..., None]
    ).astype(jnp.bfloat16)
    incoming_keys = apply_rotary(
        root_mean_scale(key_raw.astype(jnp.float32), key_norm_weight), position[..., None]
    ).astype(jnp.bfloat16).reshape(row_count, step_count, kv_heads * head_dim)
    owned_here = owner_shard == shard_id
    pad = 128
    widen = ((0, 0), (0, pad - step_count), (0, 0))
    live = jnp.pad(owned_here.astype(jnp.int32), ((0, 0), (0, pad - step_count)))
    live = jnp.broadcast_to(live[:, None, :], (row_count, 8, pad))
    here = cache_len - shard_id * span_len
    packed_rows = step_count * query_heads
    wide_dim = kv_heads * head_dim
    slot_block = lambda *shape: pl.BlockSpec((1,) + shape, lambda i, *_: (i,) + (0,) * len(shape))
    out_type = jax.ShapeDtypeStruct((row_count, packed_rows, head_dim), jnp.float32)
    block_out, block_max, block_sum = pl.pallas_call(
        functools.partial(attention_kernel, kv_heads, query_heads),
        out_shape=(out_type,) * 3,
        grid_spec=pltpu.PrefetchScalarGridSpec(
            num_scalar_prefetch=1,
            grid=(row_count,),
            in_specs=[
                slot_block(8, pad),
                slot_block(packed_rows, head_dim),
                slot_block(span_len, wide_dim),
                slot_block(span_len, wide_dim),
                slot_block(pad, wide_dim),
                slot_block(pad, wide_dim),
            ],
            out_specs=[slot_block(packed_rows, head_dim)] * 3,
        ),
    )(
        here,
        live,
        queries.reshape(row_count, packed_rows, head_dim),
        cache_keys,
        stored_values,
        jnp.pad(incoming_keys, widen),
        jnp.pad(incoming_values, widen),
    )
    split = lambda a: a.reshape(all_rows, shard_count, heads_here, -1)
    stats = jnp.concatenate([split(block_max)[..., :1], split(block_sum)[..., :1]], axis=-1)
    payload = jnp.concatenate(
        [
            split(block_out).reshape(all_rows, shard_count, -1),
            stats.reshape(all_rows, shard_count, -1),
        ],
        axis=-1,
    )
    traded = lax.all_to_all(payload, "seq", split_axis=1, concat_axis=0, tiled=False)
    wide_out = heads_here * head_dim
    outs = traded[..., :wide_out].reshape(shard_count, all_rows, heads_here, head_dim)
    stats = traded[..., wide_out:].reshape(shard_count, all_rows, heads_here, 2)
    top = jnp.max(stats[..., 0], axis=0)
    factor = jnp.exp(stats[..., 0] - top)
    numer = jnp.sum(factor[..., None] * outs, axis=0)
    denom = jnp.sum(factor * stats[..., 1], axis=0)
    attended = (numer / denom[..., None]).astype(jnp.bfloat16).reshape(all_rows, wide_out)
    group_count = lax.axis_size("req")
    rows_here = all_rows // shard_count
    if row_count == shard_count and shard_count % 2 == 0:
        own_rows = lax.dynamic_slice_in_dim(current, shard_id * rows_here, rows_here, 0)
        outputs = run_tail(
            attended, own_rows, mlp_gain.reshape(1, -1), w_out, w_gate, w_up, w_down,
            group_count, shard_count, step_count,
        )
    else:
        projected = lax.psum_scatter(
            jnp.dot(attended, w_out, preferred_element_type=jnp.float32),
            "seq",
            scatter_dimension=0,
            tiled=True,
        )
        residual = projected + lax.dynamic_slice_in_dim(current, shard_id * rows_here, rows_here, 0)
        mlp_in = root_mean_scale(residual, mlp_gain).astype(jnp.bfloat16)
        piece = lax.all_gather(mlp_in, ("req", "seq"), axis=0, tiled=True)
        gate_part = jnp.dot(piece, w_gate, preferred_element_type=jnp.float32)
        up_part = jnp.dot(piece, w_up, preferred_element_type=jnp.float32)
        hidden = (jax.nn.silu(gate_part) * up_part).astype(jnp.bfloat16)
        down = lax.psum_scatter(
            jnp.dot(hidden, w_down, preferred_element_type=jnp.float32),
            ("req", "seq"),
            scatter_dimension=0,
            tiled=True,
        )
        finished = (residual + down).astype(jnp.bfloat16)
        outputs = lax.all_gather(finished, "seq", axis=0, tiled=True)
        outputs = outputs.reshape(row_count, step_count, model_width)
    stacked_incoming = jnp.concatenate([incoming_keys, incoming_values], axis=-1)
    appended = jnp.where(owned_here[..., None], stacked_incoming, jnp.zeros((), jnp.bfloat16))
    return (outputs, appended[:, None])


def solution(mesh):
    in_specs = (
        P("req", None, None),
        P(),
        P("req"),
        P("req", None),
        P("req", "seq", None),
        P("req", "seq", None),
        P(),
        P(None, "seq"),
        P(None, "seq"),
        P(None, "seq"),
        P(),
        P(),
        P("seq", None),
        P(),
        P(None, ("req", "seq")),
        P(None, ("req", "seq")),
        P(("req", "seq"), None),
    )
    out_specs = (P("req", None, None), P("req", "seq", None, None))
    return jax.shard_map(body, mesh=mesh, in_specs=in_specs, out_specs=out_specs, check_vma=False)
```

```python
import functools
import math

import jax
import jax.numpy as jnp
from jax import lax
from jax.experimental import pallas as pl
from jax.experimental.pallas import tpu as pltpu
from jax.sharding import PartitionSpec as P

EPSILON = 1e-06
ROPE_BASE = 1000000.0
MASKED = -1e30


def root_mean_scale(tensor, gain_vec):
    mean_square = jnp.mean(tensor * tensor, axis=-1, keepdims=True)
    return tensor * lax.rsqrt(mean_square + EPSILON) * gain_vec


def apply_rotary(tensor, positions):
    half_dim = tensor.shape[-1] // 2
    frequency = ROPE_BASE ** (-2.0 * jnp.arange(half_dim, dtype=jnp.float32) / tensor.shape[-1])
    angles = positions[..., None] * frequency
    cosine = jnp.cos(angles)
    sine_part = jnp.sin(angles)
    front_half = tensor[..., :half_dim]
    back_half = tensor[..., half_dim:]
    return jnp.concatenate(
        [front_half * cosine - back_half * sine_part, back_half * cosine + front_half * sine_part],
        axis=-1,
    )


def attention_kernel(kv_heads, query_heads, here_ref, live_ref, q_ref, k_ref, v_ref, fk_ref, fv_ref,
                     out_ref, max_ref, sum_ref):
    slot = pl.program_id(0)
    rows, head_dim = q_ref.shape[1], q_ref.shape[2]
    span = k_ref.shape[1]
    pad = fk_ref.shape[1]
    width = kv_heads * head_dim
    group = query_heads // kv_heads
    scale = 1.0 / math.sqrt(head_dim)
    own_kv = lax.rem(lax.broadcasted_iota(jnp.int32, (rows, width), 0), query_heads) // group
    lane_kv = lax.broadcasted_iota(jnp.int32, (rows, width), 1) // head_dim
    q = q_ref[0]
    wide = jnp.where(own_kv == lane_kv, jnp.concatenate([q] * kv_heads, axis=1), jnp.zeros((), q.dtype))
    nt = (((1,), (1,)), ((), ()))
    scores = lax.dot_general(wide, k_ref[0], nt, preferred_element_type=jnp.float32) * scale
    in_cache = lax.broadcasted_iota(jnp.int32, (rows, span), 1) < here_ref[slot]
    scores = jnp.where(in_cache, scores, MASKED)
    fresh = lax.dot_general(wide, fk_ref[0], nt, preferred_element_type=jnp.float32) * scale
    step_row = lax.broadcasted_iota(jnp.int32, (rows, pad), 0) // query_heads
    step_lane = lax.broadcasted_iota(jnp.int32, (rows, pad), 1)
    live = (step_lane <= step_row) & (live_ref[0, 0:1, :] > 0)
    fresh = jnp.where(live, fresh, MASKED)
    top = jnp.maximum(
        jnp.max(scores, axis=1, keepdims=True), jnp.max(fresh, axis=1, keepdims=True)
    )
    weights = jnp.where(in_cache, jnp.exp(scores - top), 0.0)
    fresh_weights = jnp.where(live, jnp.exp(fresh - top), 0.0)
    total = jnp.sum(weights, axis=1, keepdims=True) + jnp.sum(fresh_weights, axis=1, keepdims=True)
    product = jnp.dot(weights.astype(jnp.bfloat16), v_ref[0], preferred_element_type=jnp.float32)
    product = product + jnp.dot(
        fresh_weights.astype(jnp.bfloat16), fv_ref[0], preferred_element_type=jnp.float32
    )
    product = jnp.where(own_kv == lane_kv, product, 0.0)
    picked = product[:, :head_dim]
    for head in range(1, kv_heads):
        picked = picked + product[:, head * head_dim:(head + 1) * head_dim]
    out_ref[0] = picked
    max_ref[0] = jnp.broadcast_to(top, (rows, head_dim))
    sum_ref[0] = jnp.broadcast_to(total, (rows, head_dim))


def layer_kernel(ring, plane, steps, slot_ref, length_ref, owner_ref, tokens_ref, attn_gain_ref, query_gain_ref,
                 key_gain_ref, cosine_ref, sine_ref, gain_ref, query_hbm, key_hbm, value_hbm, keys_hbm, stored_hbm,
                 w_out_hbm, gate_hbm, up_hbm, down_hbm, out_ref, incoming_ref, w_query, w_key, w_value, keys, stored,
                 w_out, w_gate, w_up, w_down, raw_send, raw_land, token_send, token_land, fresh, part_send,
                 part_land, stat_send, stat_land, proj_send, proj_land, mlp_all, half_send,
                 half_land, quad_send, quad_land, ring_send, ring_land, final, weight_sem, cache_sem, send_sem,
                 recv_sem):
    group = lax.axis_index("req")
    shard = lax.axis_index("seq")
    chips = plane // 2
    core, chip = lax.rem(shard, 2), shard // 2
    other = 1 - core
    partner = chip * 2 + other
    order = core * chips + chip
    mesh_type = pl.DeviceIdType.MESH
    bf16, f32 = jnp.bfloat16, jnp.float32
    nt = (((1,), (1,)), ((), ()))
    iota = lambda shape, axis: lax.broadcasted_iota(jnp.int32, shape, axis)

    plane_peers = [lax.rem(shard + d, plane) for d in range(1, plane)]
    ring_peers = [lax.rem(group + d, ring) for d in range(1, ring)]
    chip_peers = [lax.rem(chip + d, chips) * 2 + core for d in range(1, chips)]
    barrier = pltpu.get_barrier_semaphore()
    for peer in plane_peers:
        pl.semaphore_signal(barrier, inc=1, device_id=(group, peer), device_id_type=mesh_type)
    for peer in ring_peers:
        pl.semaphore_signal(barrier, inc=1, device_id=(peer, shard), device_id_type=mesh_type)
    loads = [
        pltpu.make_async_copy(src, dst, weight_sem.at[i])
        for i, (src, dst) in enumerate(
            (
                (query_hbm, w_query), (key_hbm, w_key), (value_hbm, w_value),
                (w_out_hbm, w_out), (gate_hbm, w_gate), (up_hbm, w_up), (down_hbm, w_down),
            )
        )
    ]
    slots = keys.shape[0]
    cached = [
        (
            pltpu.make_async_copy(keys_hbm.at[j], keys.at[j], cache_sem.at[0, j]),
            pltpu.make_async_copy(stored_hbm.at[j], stored.at[j], cache_sem.at[1, j]),
        )
        for j in range(slots)
    ]
    for copy in loads[:3]:
        copy.start()
    for pair in cached:
        pair[0].start()
        pair[1].start()
    for copy in loads[3:]:
        copy.start()
    weights = loads[3:]
    used = [0]
    sent = []

    def send(src, dst, device):
        index = used[0]
        used[0] += 1
        copy = pltpu.make_async_remote_copy(
            src_ref=src, dst_ref=dst, send_sem=send_sem.at[index], recv_sem=recv_sem.at[index],
            device_id=device, device_id_type=mesh_type,
        )
        copy.start()
        sent.append(copy)
        return copy

    local, _, width = tokens_ref.shape
    head_dim = query_gain_ref.shape[1]
    rows = slots * steps
    group_size = w_query.shape[1] // head_dim
    flat = tokens_ref[...].astype(f32).reshape(local * steps, width)
    normed = root_mean_scale(flat, attn_gain_ref[...]).astype(bf16)
    flat = flat.astype(bf16)
    tall, short = ring * rows, ring * steps
    slot_row, slot_lane = iota((tall, local * steps), 0), iota((tall, local * steps), 1)
    own_row, own_lane = iota((short, local * steps), 0), iota((short, local * steps), 1)
    pick = jnp.zeros((tall, local * steps), f32)
    pick_own = jnp.zeros((short, local * steps), f32)
    for i in range(local):
        slot = slot_ref[group * local + i]
        pick = jnp.where((slot_lane // steps == i) & (slot_row // steps == slot), 1.0, pick)
        pick_own = jnp.where(
            (own_lane // steps == i) & (own_row // steps * slots + shard == slot), 1.0, pick_own
        )
    pick = jnp.where(slot_row % steps == slot_lane % steps, pick, 0.0).astype(bf16)
    pick_own = jnp.where(own_row % steps == own_lane % steps, pick_own, 0.0).astype(bf16)
    raw = []
    for copy, matrix in zip(loads[:3], (w_query, w_key, w_value)):
        copy.wait()
        raw.append(jnp.dot(normed, matrix[...], preferred_element_type=f32).astype(bf16))
    raw = jnp.dot(pick, jnp.concatenate(raw, axis=1), preferred_element_type=f32).astype(bf16)
    for target in range(ring):
        raw_send[target] = raw[target * rows:(target + 1) * rows]
    pl.semaphore_wait(barrier, plane - 1 + ring - 1)
    copies = [send(raw_send.at[peer], raw_land.at[d], (peer, shard)) for d, peer in enumerate(ring_peers)]
    chosen = jnp.dot(pick_own, flat, preferred_element_type=f32)
    for target in range(ring):
        token_send[target] = chosen[target * steps:(target + 1) * steps].astype(bf16)
    token_copies = [
        send(token_send.at[peer], token_land.at[d], (peer, shard)) for d, peer in enumerate(ring_peers)
    ]
    raw = raw_send[group].astype(f32)
    for d, copy in enumerate(copies):
        copy.wait_recv()
        raw = raw + raw_land[d].astype(f32)
    cosine, sine = cosine_ref[...], sine_ref[...]

    def turned(tensor, gain_vec):
        scaled = root_mean_scale(tensor, gain_vec)
        return scaled * cosine + pltpu.roll(scaled, head_dim // 2, 1) * sine

    heads = [turned(raw[:, g * head_dim:(g + 1) * head_dim], query_gain_ref[...]) for g in range(group_size)]
    packed = rows * group_size
    by_head = jnp.concatenate(heads, axis=0).astype(bf16)
    row, lane = iota((packed, packed), 0), iota((packed, packed), 1)
    swap = jnp.where(lane == row % group_size * rows + row // group_size, 1.0, 0.0).astype(bf16)
    back = jnp.where(lane == row % rows * group_size + row // rows, 1.0, 0.0).astype(bf16)
    fresh[order, :packed] = jnp.dot(swap, by_head, preferred_element_type=f32).astype(bf16)
    key_at, value_at = packed, packed + rows
    wide = group_size * head_dim
    fresh[order, key_at:value_at] = turned(raw[:, wide:wide + head_dim], key_gain_ref[...]).astype(bf16)
    fresh[order, value_at:] = raw[:, wide + head_dim:].astype(bf16)
    own = fresh.at[order]
    copies = [send(own, own, (group, peer)) for peer in chip_peers]
    across = [send(own, own, (group, partner))]
    for d, copy in enumerate(copies):
        copy.wait_recv()
        came = fresh.at[core * chips + lax.rem(chip + chips - (d + 1), chips)]
        across.append(send(came, came, (group, partner)))
    for copy in across:
        copy.wait_recv()

    place = [(k % 2) * chips + k // 2 for k in range(plane)]
    new_keys = jnp.concatenate([fresh[p, key_at:value_at] for p in place], axis=1)
    new_values = jnp.concatenate([fresh[p, value_at:] for p in place], axis=1)
    incoming_ref[:, :plane * head_dim] = new_keys
    incoming_ref[:, plane * head_dim:] = new_values
    span = keys.shape[1]
    block = steps * group_size
    scale = 1.0 / math.sqrt(head_dim)
    all_queries = plane * block
    position = iota((all_queries, span), 1)
    step_row = iota((all_queries, rows), 0) % block // group_size
    fresh_lane = iota((all_queries, rows), 1)
    stat_lane = iota((all_queries, 128), 1)
    stats = jnp.zeros((all_queries, 128), f32)
    empty = jnp.zeros((block, head_dim), bf16)
    pair_dim = 2 * head_dim
    halves = 2
    part_copies = []
    for j in range(slots):
        cached[j][0].wait()
        pieces, new_pieces = [], []
        for k in range(0, plane, 2):
            first = fresh[place[k], j * block:(j + 1) * block]
            second = fresh[place[k + 1], j * block:(j + 1) * block]
            both = jnp.concatenate(
                [jnp.concatenate([first, empty], axis=1), jnp.concatenate([empty, second], axis=1)], axis=0
            )
            lanes = slice(k * head_dim, k * head_dim + pair_dim)
            pieces.append(lax.dot_general(both, keys[j, :, lanes], nt, preferred_element_type=f32))
            new_pieces.append(lax.dot_general(both, new_keys[:, lanes], nt, preferred_element_type=f32))
        in_cache = position < length_ref[j] - shard * span
        scores = jnp.where(in_cache, jnp.concatenate(pieces, axis=0) * scale, MASKED)
        live = fresh_lane < 0
        for t in range(steps):
            target = jnp.where(owner_ref[j, t] == shard, j * steps + t, -1)
            live = live | ((fresh_lane == target) & (step_row >= t))
        new_scores = jnp.where(live, jnp.concatenate(new_pieces, axis=0) * scale, MASKED)
        top = jnp.maximum(
            jnp.max(scores, axis=1, keepdims=True), jnp.max(new_scores, axis=1, keepdims=True)
        )
        portions = jnp.where(in_cache, jnp.exp(scores - top), 0.0)
        new_portions = jnp.where(live, jnp.exp(new_scores - top), 0.0)
        total = jnp.sum(portions, axis=1, keepdims=True) + jnp.sum(new_portions, axis=1, keepdims=True)
        portions, new_portions = portions.astype(bf16), new_portions.astype(bf16)
        stats = jnp.where(stat_lane == j, top, jnp.where(stat_lane == slots + j, total, stats))
        cached[j][1].wait()
        for k in range(0, plane, 2):
            lanes = slice(k * head_dim, k * head_dim + pair_dim)
            span_rows = slice(k * block, (k + 2) * block)
            product = jnp.dot(portions[span_rows], stored[j, :, lanes], preferred_element_type=f32)
            product = product + jnp.dot(
                new_portions[span_rows], new_values[:, lanes], preferred_element_type=f32
            )
            at = slice(j * block, (j + 1) * block)
            part_send[k, at] = product[:block, :head_dim].astype(bf16)
            part_send[k + 1, at] = product[block:, head_dim:].astype(bf16)
        if (j + 1) % (slots // halves) == 0:
            cut = pl.ds((j + 1 - slots // halves) * block, slots // halves * block)
            for d, peer in enumerate(plane_peers):
                part_copies.append(
                    send(part_send.at[peer, cut], part_land.at[d, cut], (group, peer))
                )
    stat_send[...] = jnp.transpose(stats)[:2 * slots]
    stat_copies = [send(stat_send, stat_land.at[d], (group, peer)) for d, peer in enumerate(plane_peers)]
    for copy in stat_copies:
        copy.wait_recv()
    tops = [stat_send[:slots]] + [stat_land[d, :slots] for d in range(plane - 1)]
    sums = [stat_send[slots:]] + [stat_land[d, slots:] for d in range(plane - 1)]
    joint = functools.reduce(jnp.maximum, tops)
    factors = [jnp.exp(value - joint) for value in tops]
    denom = functools.reduce(jnp.add, [f * s for f, s in zip(factors, sums)])
    here = iota((packed, 128), 1) == iota((packed, 128), 0) % block + shard * block
    columns = []
    for factor in factors:
        spread = jnp.broadcast_to((factor / denom)[:, None, :], (slots, block, 128)).reshape(packed, 128)
        columns.append(jnp.sum(jnp.where(here, spread, 0.0), axis=1, keepdims=True))
    for copy in part_copies:
        copy.wait_recv()
    blended = columns[0] * part_send[shard].astype(f32)
    for d in range(plane - 1):
        blended = blended + columns[d + 1] * part_land[d].astype(f32)
    blended = jnp.dot(back, blended.astype(bf16), preferred_element_type=f32).astype(bf16)
    attended = jnp.concatenate([blended[g * rows:(g + 1) * rows] for g in range(group_size)], axis=1)
    current = token_send[group].astype(f32)
    for d, copy in enumerate(token_copies):
        copy.wait_recv()
        current = current + token_land[d].astype(f32)

    weights[0].wait()
    projected = jnp.dot(attended, w_out[...], preferred_element_type=jnp.float32)
    for target in range(plane):
        proj_send[target] = projected[target * steps:(target + 1) * steps].astype(jnp.bfloat16)
    copies = [
        send(proj_send.at[peer], proj_land.at[d], (group, peer))
        for d, peer in enumerate(plane_peers)
    ]
    residual = current + proj_send[shard].astype(jnp.float32)
    for d, copy in enumerate(copies):
        copy.wait_recv()
        residual = residual + proj_land[d].astype(jnp.float32)
    mlp_all[order, group] = root_mean_scale(residual, gain_ref[...]).astype(jnp.bfloat16)

    own = mlp_all.at[order, group]
    copies = [send(own, own, (peer, shard)) for peer in ring_peers]
    for copy in copies:
        copy.wait_recv()
    own = mlp_all.at[order]
    copies = [send(own, own, (group, peer)) for peer in chip_peers]
    across = [send(own, own, (group, partner))]
    for d, copy in enumerate(copies):
        copy.wait_recv()
        came = mlp_all.at[core * chips + lax.rem(chip + chips - (d + 1), chips)]
        across.append(send(came, came, (group, partner)))
    for copy in across:
        copy.wait_recv()

    width = mlp_all.shape[-1]
    rows = plane * ring * steps
    mlp_in = mlp_all[...].astype(jnp.float32).reshape(rows, width).astype(jnp.bfloat16)
    weights[1].wait()
    gate_part = lax.dot_general(mlp_in, w_gate[...], nt, preferred_element_type=jnp.float32)
    weights[2].wait()
    up_part = lax.dot_general(mlp_in, w_up[...], nt, preferred_element_type=jnp.float32)
    hidden = (gate_part / (1.0 + jnp.exp(-gate_part)) * up_part).astype(jnp.bfloat16)
    weights[3].wait()
    down = jnp.dot(hidden, w_down[...], preferred_element_type=jnp.float32)
    half = rows // 2
    half_send[0] = down[:half].astype(jnp.bfloat16)
    half_send[1] = down[half:].astype(jnp.bfloat16)
    copy = send(half_send.at[other], half_land, (group, partner))
    copy.wait_recv()
    both = half_send[core].astype(jnp.float32) + half_land[...].astype(jnp.float32)
    quad = ring * steps
    for target in range(chips):
        quad_send[target] = both[target * quad:(target + 1) * quad].astype(jnp.bfloat16)
    copies = [
        send(quad_send.at[peer // 2], quad_land.at[d], (group, peer))
        for d, peer in enumerate(chip_peers)
    ]
    summed = quad_send[chip].astype(jnp.float32)
    for d, copy in enumerate(copies):
        copy.wait_recv()
        summed = summed + quad_land[d].astype(jnp.float32)
    for target in range(ring):
        ring_send[target] = summed[target * steps:(target + 1) * steps].astype(jnp.bfloat16)
    copies = [
        send(ring_send.at[peer], ring_land.at[d], (peer, shard)) for d, peer in enumerate(ring_peers)
    ]
    total = residual + ring_send[group].astype(jnp.float32)
    for d, copy in enumerate(copies):
        copy.wait_recv()
        total = total + ring_land[d].astype(jnp.float32)
    final[shard] = total.astype(jnp.bfloat16)
    own = final.at[shard]
    copies = [send(own, own, (group, peer)) for peer in plane_peers]
    for copy in copies:
        copy.wait_recv()
    out_ref[...] = final[...]
    for copy in sent:
        copy.wait_send()


def run_layer(scalars, vectors, matrices, ring, plane, steps):
    tokens = vectors[0]
    w_query, key_matrix, value_matrix, cache_keys, stored_values, w_out, w_gate, w_up, w_down = matrices
    width = w_out.shape[1]
    head_dim = key_matrix.shape[1]
    slots = cache_keys.shape[0]
    all_rows = plane * ring * steps
    rows = slots * steps
    packed = rows * (w_query.shape[1] // head_dim)
    made = w_query.shape[1] + 2 * head_dim
    chips = plane // 2
    bf16, f32 = jnp.bfloat16, jnp.float32
    copies = 5 * (plane - 1) + 5 * (ring - 1) + 5 * chips + 8
    vmem = pl.BlockSpec(memory_space=pltpu.VMEM)
    smem = pl.BlockSpec(memory_space=pltpu.SMEM)
    anywhere = pl.BlockSpec(memory_space=pl.ANY)
    return pl.pallas_call(
        functools.partial(layer_kernel, ring, plane, steps),
        out_shape=(
            jax.ShapeDtypeStruct((plane, steps, width), bf16),
            jax.ShapeDtypeStruct((rows, 2 * plane * head_dim), bf16),
        ),
        in_specs=[smem] * len(scalars) + [vmem] * len(vectors) + [anywhere] * len(matrices),
        out_specs=(vmem, vmem),
        scratch_shapes=[pltpu.VMEM(matrix.shape, bf16) for matrix in matrices] + [
            pltpu.VMEM((ring, rows, made), bf16),
            pltpu.VMEM((ring - 1, rows, made), bf16),
            pltpu.VMEM((ring, steps, width), bf16),
            pltpu.VMEM((ring - 1, steps, width), bf16),
            pltpu.VMEM((plane, packed + 2 * rows, head_dim), bf16),
            pltpu.VMEM((plane, packed, head_dim), bf16),
            pltpu.VMEM((plane - 1, packed, head_dim), bf16),
            pltpu.VMEM((2 * slots, 128), f32),
            pltpu.VMEM((plane - 1, 2 * slots, 128), f32),
            pltpu.VMEM((plane, steps, width), bf16),
            pltpu.VMEM((plane - 1, steps, width), bf16),
            pltpu.VMEM((plane, ring, steps, width), bf16),
            pltpu.VMEM((2, all_rows // 2, width), bf16),
            pltpu.VMEM((all_rows // 2, width), bf16),
            pltpu.VMEM((chips, ring * steps, width), bf16),
            pltpu.VMEM((chips - 1, ring * steps, width), bf16),
            pltpu.VMEM((ring, steps, width), bf16),
            pltpu.VMEM((ring - 1, steps, width), bf16),
            pltpu.VMEM((plane, steps, width), bf16),
            pltpu.SemaphoreType.DMA((7,)),
            pltpu.SemaphoreType.DMA((2, slots)),
            pltpu.SemaphoreType.DMA((copies,)),
            pltpu.SemaphoreType.DMA((copies,)),
        ],
        compiler_params=pltpu.CompilerParams(collective_id=0, has_side_effects=True),
    )(*scalars, *vectors, *matrices)


def whole_layer(
    tokens,
    slot_of,
    cache_len,
    owner_shard,
    cache_keys,
    stored_values,
    attn_gain,
    w_query,
    key_matrix,
    value_matrix,
    query_gain,
    key_norm_weight,
    w_out,
    mlp_gain,
    w_gate,
    w_up,
    w_down,
):
    plane, ring = lax.axis_size("seq"), lax.axis_size("req")
    slots, steps = owner_shard.shape
    head_dim = query_gain.shape[0]
    half = head_dim // 2
    position = (cache_len[:, None] + jnp.arange(steps, dtype=jnp.int32)).astype(jnp.float32)
    frequency = ROPE_BASE ** (-2.0 * jnp.arange(half, dtype=jnp.float32) / head_dim)
    angles = position.reshape(-1, 1) * frequency
    cosine, sine = jnp.cos(angles), jnp.sin(angles)
    outputs, incoming = run_layer(
        (slot_of, cache_len, owner_shard),
        (
            tokens,
            attn_gain.reshape(1, -1),
            query_gain.reshape(1, -1),
            key_norm_weight.reshape(1, -1),
            jnp.concatenate([cosine, cosine], axis=1),
            jnp.concatenate([-sine, sine], axis=1),
            mlp_gain.reshape(1, -1),
        ),
        (
            w_query, key_matrix, value_matrix, cache_keys, stored_values, w_out,
            w_gate.T, w_up.T, w_down,
        ),
        ring, plane, steps,
    )
    owned_here = owner_shard == lax.axis_index("seq")
    incoming = incoming.reshape(slots, steps, -1)
    appended = jnp.where(owned_here[..., None], incoming, jnp.zeros((), jnp.bfloat16))
    return (outputs, appended[:, None])


def body(
    tokens,
    slot_of,
    cache_len,
    owner_shard,
    cache_keys,
    stored_values,
    attn_gain,
    w_query,
    key_matrix,
    value_matrix,
    query_gain,
    key_norm_weight,
    w_out,
    mlp_gain,
    w_gate,
    w_up,
    w_down,
):
    group_id = lax.axis_index("req")
    shard_id = lax.axis_index("seq")
    shard_count = lax.axis_size("seq")
    row_count = cache_len.shape[0]
    span_len = cache_keys.shape[1]
    step_count, model_width = tokens.shape[1:]
    head_dim = query_gain.shape[0]
    kv_heads = cache_keys.shape[2] // head_dim
    query_heads = w_query.shape[1] * shard_count // head_dim
    heads_here = query_heads // shard_count
    all_rows = row_count * step_count
    arrived = lax.all_gather(tokens, "req", axis=0, tiled=True)
    slot_ids = group_id * row_count + jnp.arange(row_count, dtype=jnp.int32)
    selector = (slot_of[None, :] == slot_ids[:, None]).astype(jnp.bfloat16)
    inputs = jnp.einsum("ji,isd->jsd", selector, arrived, preferred_element_type=jnp.float32)
    current = inputs.reshape(all_rows, model_width)
    normed = root_mean_scale(current, attn_gain).astype(jnp.bfloat16)
    parts = [
        jnp.dot(normed, matrix, preferred_element_type=jnp.float32).astype(jnp.bfloat16)
        for matrix in (w_query, key_matrix, value_matrix)
    ]
    cut = [parts[0].shape[1], parts[0].shape[1] + parts[1].shape[1]]
    gathered = lax.all_gather(jnp.concatenate(parts, axis=1), "seq", axis=0)
    gathered = jnp.transpose(gathered, (1, 0, 2))
    query_raw = gathered[:, :, :cut[0]].reshape(row_count, step_count, query_heads, head_dim)
    key_raw = gathered[:, :, cut[0]:cut[1]].reshape(row_count, step_count, kv_heads, head_dim)
    incoming_values = gathered[:, :, cut[1]:].reshape(row_count, step_count, kv_heads * head_dim)
    position = (cache_len[:, None] + jnp.arange(step_count, dtype=jnp.int32)).astype(jnp.float32)
    queries = apply_rotary(
        root_mean_scale(query_raw.astype(jnp.float32), query_gain), position[..., None]
    ).astype(jnp.bfloat16)
    incoming_keys = apply_rotary(
        root_mean_scale(key_raw.astype(jnp.float32), key_norm_weight), position[..., None]
    ).astype(jnp.bfloat16).reshape(row_count, step_count, kv_heads * head_dim)
    owned_here = owner_shard == shard_id
    pad = 128
    widen = ((0, 0), (0, pad - step_count), (0, 0))
    live = jnp.pad(owned_here.astype(jnp.int32), ((0, 0), (0, pad - step_count)))
    live = jnp.broadcast_to(live[:, None, :], (row_count, 8, pad))
    here = cache_len - shard_id * span_len
    packed_rows = step_count * query_heads
    wide_dim = kv_heads * head_dim
    slot_block = lambda *shape: pl.BlockSpec((1,) + shape, lambda i, *_: (i,) + (0,) * len(shape))
    out_type = jax.ShapeDtypeStruct((row_count, packed_rows, head_dim), jnp.float32)
    block_out, block_max, block_sum = pl.pallas_call(
        functools.partial(attention_kernel, kv_heads, query_heads),
        out_shape=(out_type,) * 3,
        grid_spec=pltpu.PrefetchScalarGridSpec(
            num_scalar_prefetch=1,
            grid=(row_count,),
            in_specs=[
                slot_block(8, pad),
                slot_block(packed_rows, head_dim),
                slot_block(span_len, wide_dim),
                slot_block(span_len, wide_dim),
                slot_block(pad, wide_dim),
                slot_block(pad, wide_dim),
            ],
            out_specs=[slot_block(packed_rows, head_dim)] * 3,
        ),
    )(
        here,
        live,
        queries.reshape(row_count, packed_rows, head_dim),
        cache_keys,
        stored_values,
        jnp.pad(incoming_keys, widen),
        jnp.pad(incoming_values, widen),
    )
    split = lambda a: a.reshape(all_rows, shard_count, heads_here, -1)
    stats = jnp.concatenate([split(block_max)[..., :1], split(block_sum)[..., :1]], axis=-1)
    payload = jnp.concatenate(
        [
            split(block_out).reshape(all_rows, shard_count, -1),
            stats.reshape(all_rows, shard_count, -1),
        ],
        axis=-1,
    )
    traded = lax.all_to_all(payload, "seq", split_axis=1, concat_axis=0, tiled=False)
    wide_out = heads_here * head_dim
    outs = traded[..., :wide_out].reshape(shard_count, all_rows, heads_here, head_dim)
    stats = traded[..., wide_out:].reshape(shard_count, all_rows, heads_here, 2)
    top = jnp.max(stats[..., 0], axis=0)
    factor = jnp.exp(stats[..., 0] - top)
    numer = jnp.sum(factor[..., None] * outs, axis=0)
    denom = jnp.sum(factor * stats[..., 1], axis=0)
    attended = (numer / denom[..., None]).astype(jnp.bfloat16).reshape(all_rows, wide_out)
    projected = lax.psum_scatter(
        jnp.dot(attended, w_out, preferred_element_type=jnp.float32),
        "seq",
        scatter_dimension=0,
        tiled=True,
    )
    rows_here = all_rows // shard_count
    residual = projected + lax.dynamic_slice_in_dim(current, shard_id * rows_here, rows_here, 0)
    mlp_in = root_mean_scale(residual, mlp_gain).astype(jnp.bfloat16)
    piece = lax.all_gather(mlp_in, ("req", "seq"), axis=0, tiled=True)
    gate_part = jnp.dot(piece, w_gate, preferred_element_type=jnp.float32)
    up_part = jnp.dot(piece, w_up, preferred_element_type=jnp.float32)
    hidden = (jax.nn.silu(gate_part) * up_part).astype(jnp.bfloat16)
    down = lax.psum_scatter(
        jnp.dot(hidden, w_down, preferred_element_type=jnp.float32),
        ("req", "seq"),
        scatter_dimension=0,
        tiled=True,
    )
    finished = (residual + down).astype(jnp.bfloat16)
    outputs = lax.all_gather(finished, "seq", axis=0, tiled=True)
    outputs = outputs.reshape(row_count, step_count, model_width)
    stacked_incoming = jnp.concatenate([incoming_keys, incoming_values], axis=-1)
    appended = jnp.where(owned_here[..., None], stacked_incoming, jnp.zeros((), jnp.bfloat16))
    return (outputs, appended[:, None])


def solution(mesh):
    in_specs = (
        P("req", None, None),
        P(),
        P("req"),
        P("req", None),
        P("req", "seq", None),
        P("req", "seq", None),
        P(),
        P(None, "seq"),
        P(None, "seq"),
        P(None, "seq"),
        P(),
        P(),
        P("seq", None),
        P(),
        P(None, ("req", "seq")),
        P(None, ("req", "seq")),
        P(("req", "seq"), None),
    )
    out_specs = (P("req", None, None), P("req", "seq", None, None))

    def layer(*arrays):
        kv_heads = arrays[4].shape[2] // arrays[10].shape[0]
        row_count = arrays[2].shape[0]
        shards = lax.axis_size("seq")
        if row_count == shards and kv_heads == shards and shards % 2 == 0:
            return whole_layer(*arrays)
        return body(*arrays)

    return jax.shard_map(layer, mesh=mesh, in_specs=in_specs, out_specs=out_specs, check_vma=False)
```

```python
import functools
import math

import jax
import jax.numpy as jnp
from jax import lax
from jax.experimental import pallas as pl
from jax.experimental.pallas import tpu as pltpu
from jax.sharding import PartitionSpec as P

EPSILON = 1e-06
ROPE_BASE = 1000000.0
MASKED = -1e30


def root_mean_scale(tensor, gain_vec):
    mean_square = jnp.mean(tensor * tensor, axis=-1, keepdims=True)
    return tensor * lax.rsqrt(mean_square + EPSILON) * gain_vec


def apply_rotary(tensor, positions):
    half_dim = tensor.shape[-1] // 2
    frequency = ROPE_BASE ** (-2.0 * jnp.arange(half_dim, dtype=jnp.float32) / tensor.shape[-1])
    angles = positions[..., None] * frequency
    cosine = jnp.cos(angles)
    sine_part = jnp.sin(angles)
    front_half = tensor[..., :half_dim]
    back_half = tensor[..., half_dim:]
    return jnp.concatenate(
        [front_half * cosine - back_half * sine_part, back_half * cosine + front_half * sine_part],
        axis=-1,
    )


def attention_kernel(kv_heads, query_heads, here_ref, live_ref, q_ref, k_ref, v_ref, fk_ref, fv_ref,
                     out_ref, max_ref, sum_ref):
    slot = pl.program_id(0)
    rows, head_dim = q_ref.shape[1], q_ref.shape[2]
    span = k_ref.shape[1]
    pad = fk_ref.shape[1]
    width = kv_heads * head_dim
    group = query_heads // kv_heads
    scale = 1.0 / math.sqrt(head_dim)
    own_kv = lax.rem(lax.broadcasted_iota(jnp.int32, (rows, width), 0), query_heads) // group
    lane_kv = lax.broadcasted_iota(jnp.int32, (rows, width), 1) // head_dim
    q = q_ref[0]
    wide = jnp.where(own_kv == lane_kv, jnp.concatenate([q] * kv_heads, axis=1), jnp.zeros((), q.dtype))
    nt = (((1,), (1,)), ((), ()))
    scores = lax.dot_general(wide, k_ref[0], nt, preferred_element_type=jnp.float32) * scale
    in_cache = lax.broadcasted_iota(jnp.int32, (rows, span), 1) < here_ref[slot]
    scores = jnp.where(in_cache, scores, MASKED)
    fresh = lax.dot_general(wide, fk_ref[0], nt, preferred_element_type=jnp.float32) * scale
    step_row = lax.broadcasted_iota(jnp.int32, (rows, pad), 0) // query_heads
    step_lane = lax.broadcasted_iota(jnp.int32, (rows, pad), 1)
    live = (step_lane <= step_row) & (live_ref[0, 0:1, :] > 0)
    fresh = jnp.where(live, fresh, MASKED)
    top = jnp.maximum(
        jnp.max(scores, axis=1, keepdims=True), jnp.max(fresh, axis=1, keepdims=True)
    )
    weights = jnp.where(in_cache, jnp.exp(scores - top), 0.0)
    fresh_weights = jnp.where(live, jnp.exp(fresh - top), 0.0)
    total = jnp.sum(weights, axis=1, keepdims=True) + jnp.sum(fresh_weights, axis=1, keepdims=True)
    product = jnp.dot(weights.astype(jnp.bfloat16), v_ref[0], preferred_element_type=jnp.float32)
    product = product + jnp.dot(
        fresh_weights.astype(jnp.bfloat16), fv_ref[0], preferred_element_type=jnp.float32
    )
    product = jnp.where(own_kv == lane_kv, product, 0.0)
    picked = product[:, :head_dim]
    for head in range(1, kv_heads):
        picked = picked + product[:, head * head_dim:(head + 1) * head_dim]
    out_ref[0] = picked
    max_ref[0] = jnp.broadcast_to(top, (rows, head_dim))
    sum_ref[0] = jnp.broadcast_to(total, (rows, head_dim))


def unfolded(folded_ref):
    folded = folded_ref[...]
    return jnp.concatenate([folded[i:i + 1] for i in range(folded.shape[0])], axis=1)


def layer_kernel(ring, plane, steps, slot_ref, length_ref, owner_ref, tokens_ref, attn_gain_ref, query_gain_ref,
                 key_gain_ref, cosine_ref, sine_ref, gain_ref, query_hbm, key_hbm, value_hbm, keys_hbm, stored_hbm,
                 w_out_hbm, gate_hbm, up_hbm, down_hbm, out_ref, incoming_ref, w_query, w_key, w_value, keys, stored,
                 w_out, w_gate, w_up, w_down, raw_send, raw_land, token_send, token_land, fresh, part_send,
                 part_land, stat_send, stat_land, proj_send, proj_land, mlp_all, hidden_ref,
                 half_send, half_land, quad_send, quad_land, ring_send, ring_land, final, weight_sem, cache_sem, send_sem,
                 recv_sem):
    group = lax.axis_index("req")
    shard = lax.axis_index("seq")
    chips = plane // 2
    core, chip = lax.rem(shard, 2), shard // 2
    other = 1 - core
    partner = chip * 2 + other
    order = core * chips + chip
    mesh_type = pl.DeviceIdType.MESH
    bf16, f32 = jnp.bfloat16, jnp.float32
    nt = (((1,), (1,)), ((), ()))
    iota = lambda shape, axis: lax.broadcasted_iota(jnp.int32, shape, axis)

    plane_peers = [lax.rem(shard + d, plane) for d in range(1, plane)]
    ring_peers = [lax.rem(group + d, ring) for d in range(1, ring)]
    chip_peers = [lax.rem(chip + d, chips) * 2 + core for d in range(1, chips)]
    barrier = pltpu.get_barrier_semaphore()
    for peer in plane_peers:
        pl.semaphore_signal(barrier, inc=1, device_id=(group, peer), device_id_type=mesh_type)
    for peer in ring_peers:
        pl.semaphore_signal(barrier, inc=1, device_id=(peer, shard), device_id_type=mesh_type)
    loads = [
        pltpu.make_async_copy(src, dst, weight_sem.at[i])
        for i, (src, dst) in enumerate(
            (
                (query_hbm, w_query), (key_hbm, w_key), (value_hbm, w_value),
                (w_out_hbm, w_out), (gate_hbm, w_gate), (up_hbm, w_up), (down_hbm, w_down),
            )
        )
    ]
    slots = keys.shape[0]
    cached = [
        (
            pltpu.make_async_copy(keys_hbm.at[j], keys.at[j], cache_sem.at[0, j]),
            pltpu.make_async_copy(stored_hbm.at[j], stored.at[j], cache_sem.at[1, j]),
        )
        for j in range(slots)
    ]
    for copy in loads[:3]:
        copy.start()
    for pair in cached:
        pair[0].start()
        pair[1].start()
    for copy in loads[3:]:
        copy.start()
    weights = loads[3:]
    used = [0]
    sent = []

    def send(src, dst, device):
        index = used[0]
        used[0] += 1
        copy = pltpu.make_async_remote_copy(
            src_ref=src, dst_ref=dst, send_sem=send_sem.at[index], recv_sem=recv_sem.at[index],
            device_id=device, device_id_type=mesh_type,
        )
        copy.start()
        sent.append(copy)
        return copy

    local, _, width = tokens_ref.shape
    head_dim = query_gain_ref.shape[1]
    rows = slots * steps
    group_size = w_query.shape[1] // head_dim
    flat = tokens_ref[...].astype(f32).reshape(local * steps, width)
    normed = root_mean_scale(flat, unfolded(attn_gain_ref)).astype(bf16)
    flat = flat.astype(bf16)
    tall, short = ring * rows, ring * steps
    slot_row, slot_lane = iota((tall, local * steps), 0), iota((tall, local * steps), 1)
    own_row, own_lane = iota((short, local * steps), 0), iota((short, local * steps), 1)
    pick = jnp.zeros((tall, local * steps), f32)
    pick_own = jnp.zeros((short, local * steps), f32)
    for i in range(local):
        slot = slot_ref[group * local + i]
        pick = jnp.where((slot_lane // steps == i) & (slot_row // steps == slot), 1.0, pick)
        pick_own = jnp.where(
            (own_lane // steps == i) & (own_row // steps * slots + shard == slot), 1.0, pick_own
        )
    pick = jnp.where(slot_row % steps == slot_lane % steps, pick, 0.0).astype(bf16)
    pick_own = jnp.where(own_row % steps == own_lane % steps, pick_own, 0.0).astype(bf16)
    raw = []
    for copy, matrix in zip(loads[:3], (w_query, w_key, w_value)):
        copy.wait()
        raw.append(jnp.dot(normed, matrix[...], preferred_element_type=f32).astype(bf16))
    raw = jnp.dot(pick, jnp.concatenate(raw, axis=1), preferred_element_type=f32).astype(bf16)
    for target in range(ring):
        raw_send[target] = raw[target * rows:(target + 1) * rows]
    pl.semaphore_wait(barrier, plane - 1 + ring - 1)
    copies = [send(raw_send.at[peer], raw_land.at[d], (peer, shard)) for d, peer in enumerate(ring_peers)]
    chosen = jnp.dot(pick_own, flat, preferred_element_type=f32)
    for target in range(ring):
        token_send[target] = chosen[target * steps:(target + 1) * steps].astype(bf16)
    raw = raw_send[group].astype(f32)
    for d, copy in enumerate(copies):
        copy.wait_recv()
        raw = raw + raw_land[d].astype(f32)
    token_copies = [
        send(token_send.at[peer], token_land.at[d], (peer, shard)) for d, peer in enumerate(ring_peers)
    ]
    cosine, sine = cosine_ref[...], sine_ref[...]

    def turned(tensor, gain_vec):
        scaled = root_mean_scale(tensor, gain_vec)
        return scaled * cosine + pltpu.roll(scaled, head_dim // 2, 1) * sine

    heads = [turned(raw[:, g * head_dim:(g + 1) * head_dim], query_gain_ref[...]) for g in range(group_size)]
    packed = rows * group_size
    by_head = jnp.concatenate(heads, axis=0).astype(bf16)
    row, lane = iota((packed, packed), 0), iota((packed, packed), 1)
    swap = jnp.where(lane == row % group_size * rows + row // group_size, 1.0, 0.0).astype(bf16)
    back = jnp.where(lane == row % rows * group_size + row // rows, 1.0, 0.0).astype(bf16)
    fresh[order, :packed] = jnp.dot(swap, by_head, preferred_element_type=f32).astype(bf16)
    key_at, value_at = packed, packed + rows
    wide = group_size * head_dim
    fresh[order, key_at:value_at] = turned(raw[:, wide:wide + head_dim], key_gain_ref[...]).astype(bf16)
    fresh[order, value_at:] = raw[:, wide + head_dim:].astype(bf16)
    own = fresh.at[order]
    copies = [send(own, own, (group, peer)) for peer in chip_peers]
    across = [send(own, own, (group, partner))]
    for d, copy in enumerate(copies):
        copy.wait_recv()
        came = fresh.at[core * chips + lax.rem(chip + chips - (d + 1), chips)]
        across.append(send(came, came, (group, partner)))
    for copy in across:
        copy.wait_recv()

    place = [(k % 2) * chips + k // 2 for k in range(plane)]
    new_keys = jnp.concatenate([fresh[p, key_at:value_at] for p in place], axis=1)
    new_values = jnp.concatenate([fresh[p, value_at:] for p in place], axis=1)
    span = keys.shape[1]
    block = steps * group_size
    scale = 1.0 / math.sqrt(head_dim)
    all_queries = plane * block
    position = iota((all_queries, span), 1)
    step_row = iota((all_queries, rows), 0) % block // group_size
    fresh_lane = iota((all_queries, rows), 1)
    stat_lane = iota((all_queries, 128), 1)
    stats = jnp.zeros((all_queries, 128), f32)
    empty = jnp.zeros((block, head_dim), bf16)
    pair_dim = 2 * head_dim
    halves = 4
    part_copies = []
    for j in range(slots):
        cached[j][0].wait()
        pieces, new_pieces = [], []
        for k in range(0, plane, 2):
            first = fresh[place[k], j * block:(j + 1) * block]
            second = fresh[place[k + 1], j * block:(j + 1) * block]
            both = jnp.concatenate(
                [jnp.concatenate([first, empty], axis=1), jnp.concatenate([empty, second], axis=1)], axis=0
            )
            lanes = slice(k * head_dim, k * head_dim + pair_dim)
            pieces.append(lax.dot_general(both, keys[j, :, lanes], nt, preferred_element_type=f32))
            new_pieces.append(lax.dot_general(both, new_keys[:, lanes], nt, preferred_element_type=f32))
        in_cache = position < length_ref[j] - shard * span
        scores = jnp.where(in_cache, jnp.concatenate(pieces, axis=0) * scale, MASKED)
        live = fresh_lane < 0
        for t in range(steps):
            target = jnp.where(owner_ref[t, j] == shard, j * steps + t, -1)
            live = live | ((fresh_lane == target) & (step_row >= t))
        new_scores = jnp.where(live, jnp.concatenate(new_pieces, axis=0) * scale, MASKED)
        top = jnp.maximum(
            jnp.max(scores, axis=1, keepdims=True), jnp.max(new_scores, axis=1, keepdims=True)
        )
        portions = jnp.where(in_cache, jnp.exp(scores - top), 0.0)
        new_portions = jnp.where(live, jnp.exp(new_scores - top), 0.0)
        total = jnp.sum(portions, axis=1, keepdims=True) + jnp.sum(new_portions, axis=1, keepdims=True)
        portions, new_portions = portions.astype(bf16), new_portions.astype(bf16)
        stats = jnp.where(stat_lane == j, top, jnp.where(stat_lane == slots + j, total, stats))
        cached[j][1].wait()
        for k in range(0, plane, 2):
            lanes = slice(k * head_dim, k * head_dim + pair_dim)
            span_rows = slice(k * block, (k + 2) * block)
            product = jnp.dot(portions[span_rows], stored[j, :, lanes], preferred_element_type=f32)
            product = product + jnp.dot(
                new_portions[span_rows], new_values[:, lanes], preferred_element_type=f32
            )
            at = slice(j * block, (j + 1) * block)
            part_send[k, at] = product[:block, :head_dim].astype(bf16)
            part_send[k + 1, at] = product[block:, head_dim:].astype(bf16)
        if (j + 1) % (slots // halves) == 0:
            cut = pl.ds((j + 1 - slots // halves) * block, slots // halves * block)
            for d, peer in enumerate(plane_peers):
                part_copies.append(
                    send(part_send.at[peer, cut], part_land.at[d, cut], (group, peer))
                )
    stat_send[...] = jnp.transpose(stats)[:2 * slots]
    stat_copies = [send(stat_send, stat_land.at[d], (group, peer)) for d, peer in enumerate(plane_peers)]
    for copy in stat_copies:
        copy.wait_recv()
    tops = [stat_send[:slots]] + [stat_land[d, :slots] for d in range(plane - 1)]
    sums = [stat_send[slots:]] + [stat_land[d, slots:] for d in range(plane - 1)]
    joint = functools.reduce(jnp.maximum, tops)
    factors = [jnp.exp(value - joint) for value in tops]
    denom = functools.reduce(jnp.add, [f * s for f, s in zip(factors, sums)])
    here = iota((packed, 128), 1) == iota((packed, 128), 0) % block + shard * block
    columns = []
    for factor in factors:
        spread = jnp.broadcast_to((factor / denom)[:, None, :], (slots, block, 128)).reshape(packed, 128)
        columns.append(jnp.sum(jnp.where(here, spread, 0.0), axis=1, keepdims=True))
    for copy in part_copies:
        copy.wait_recv()
    blended = columns[0] * part_send[shard].astype(f32)
    for d in range(plane - 1):
        blended = blended + columns[d + 1] * part_land[d].astype(f32)
    blended = jnp.dot(back, blended.astype(bf16), preferred_element_type=f32).astype(bf16)
    attended = jnp.concatenate([blended[g * rows:(g + 1) * rows] for g in range(group_size)], axis=1)
    current = token_send[group].astype(f32)
    for d, copy in enumerate(token_copies):
        copy.wait_recv()
        current = current + token_land[d].astype(f32)

    weights[0].wait()
    projected = jnp.dot(attended, w_out[...], preferred_element_type=jnp.float32)
    for target in range(plane):
        proj_send[target] = projected[target * steps:(target + 1) * steps].astype(jnp.bfloat16)
    copies = [
        send(proj_send.at[peer], proj_land.at[d], (group, peer))
        for d, peer in enumerate(plane_peers)
    ]
    for at, fresh_rows in ((0, new_keys), (plane * head_dim, new_values)):
        fresh_rows = fresh_rows.astype(f32)
        for j in range(slots):
            incoming_ref[j, :, at:at + plane * head_dim] = fresh_rows[j * steps:(j + 1) * steps].astype(bf16)
    residual = current + proj_send[shard].astype(jnp.float32)
    for d, copy in enumerate(copies):
        copy.wait_recv()
        residual = residual + proj_land[d].astype(jnp.float32)
    mlp_all[order, group] = root_mean_scale(residual, unfolded(gain_ref)).astype(jnp.bfloat16)

    own = mlp_all.at[order, group]
    ring_copies = [None] + [send(own, own, (peer, shard)) for peer in ring_peers]
    spread_copies, across = [], []
    for d, copy in enumerate(ring_copies):
        source = lax.rem(group + ring - d, ring)
        if copy is not None:
            copy.wait_recv()
        held = mlp_all.at[order, source]
        spread_copies.append([send(held, held, (group, peer)) for peer in chip_peers])
        across.append(send(held, held, (group, partner)))
    for d, copies in enumerate(spread_copies):
        source = lax.rem(group + ring - d, ring)
        for e, copy in enumerate(copies):
            copy.wait_recv()
            held = mlp_all.at[core * chips + lax.rem(chip + chips - (e + 1), chips), source]
            across.append(send(held, held, (group, partner)))
    for copy in across:
        copy.wait_recv()

    width = mlp_all.shape[-1]
    rows = plane * ring * steps
    mlp_in = mlp_all[...].astype(jnp.float32).reshape(rows, width).astype(jnp.bfloat16)
    weights[1].wait()
    gate_part = lax.dot_general(mlp_in, w_gate[...], nt, preferred_element_type=jnp.float32)
    weights[2].wait()
    up_part = lax.dot_general(mlp_in, w_up[...], nt, preferred_element_type=jnp.float32)
    hidden = (gate_part / (1.0 + jnp.exp(-gate_part)) * up_part).astype(jnp.bfloat16)
    weights[3].wait()
    half = rows // 2
    hidden_ref[0] = hidden[:half]
    hidden_ref[1] = hidden[half:]
    half_send[...] = jnp.dot(hidden_ref[other], w_down[...], preferred_element_type=jnp.float32).astype(
        jnp.bfloat16
    )
    copy = send(half_send, half_land, (group, partner))
    both = jnp.dot(hidden_ref[core], w_down[...], preferred_element_type=jnp.float32)
    copy.wait_recv()
    both = both + half_land[...].astype(jnp.float32)
    for target in range(chips * ring):
        quad_send[target // ring, target % ring] = both[target * steps:(target + 1) * steps].astype(
            jnp.bfloat16
        )
    targets = ring_peers + [group]
    quad_copies = [
        [
            send(quad_send.at[peer // 2, target], quad_land.at[e, target], (group, peer))
            for e, peer in enumerate(chip_peers)
        ]
        for target in targets
    ]
    ring_copies = []
    for d, target in enumerate(targets):
        summed = quad_send[chip, target].astype(jnp.float32)
        for e, copy in enumerate(quad_copies[d]):
            copy.wait_recv()
            summed = summed + quad_land[e, target].astype(jnp.float32)
        if d < ring - 1:
            ring_send[d] = summed.astype(jnp.bfloat16)
            ring_copies.append(send(ring_send.at[d], ring_land.at[d], (target, shard)))
    total = residual + summed
    for d, copy in enumerate(ring_copies):
        copy.wait_recv()
        total = total + ring_land[d].astype(jnp.float32)
    final[shard] = total.astype(jnp.bfloat16)
    own = final.at[shard]
    copies = [send(own, own, (group, peer)) for peer in plane_peers]
    for copy in copies:
        copy.wait_recv()
    out_ref[...] = final[...].astype(f32)
    for copy in sent:
        copy.wait_send()


def run_layer(scalars, vectors, matrices, ring, plane, steps):
    tokens = vectors[0]
    w_query, key_matrix, value_matrix, cache_keys, stored_values, w_out, w_gate, w_up, w_down = matrices
    width = w_out.shape[1]
    head_dim = key_matrix.shape[1]
    slots = cache_keys.shape[0]
    all_rows = plane * ring * steps
    rows = slots * steps
    packed = rows * (w_query.shape[1] // head_dim)
    made = w_query.shape[1] + 2 * head_dim
    chips = plane // 2
    bf16, f32 = jnp.bfloat16, jnp.float32
    copies = 7 * (plane - 1) + 4 * (ring - 1) + 2 * chips + ring * (3 * chips - 1) + 2
    vmem = pl.BlockSpec(memory_space=pltpu.VMEM)
    smem = pl.BlockSpec(memory_space=pltpu.SMEM)
    anywhere = pl.BlockSpec(memory_space=pl.ANY)
    return pl.pallas_call(
        functools.partial(layer_kernel, ring, plane, steps),
        out_shape=(
            jax.ShapeDtypeStruct((plane, steps, width), f32),
            jax.ShapeDtypeStruct((slots, steps, 2 * plane * head_dim), bf16),
        ),
        in_specs=[smem] * len(scalars) + [vmem] * len(vectors) + [anywhere] * len(matrices),
        out_specs=(vmem, vmem),
        scratch_shapes=[pltpu.VMEM(matrix.shape, bf16) for matrix in matrices] + [
            pltpu.VMEM((ring, rows, made), bf16),
            pltpu.VMEM((ring - 1, rows, made), bf16),
            pltpu.VMEM((ring, steps, width), bf16),
            pltpu.VMEM((ring - 1, steps, width), bf16),
            pltpu.VMEM((plane, packed + 2 * rows, head_dim), bf16),
            pltpu.VMEM((plane, packed, head_dim), bf16),
            pltpu.VMEM((plane - 1, packed, head_dim), bf16),
            pltpu.VMEM((2 * slots, 128), f32),
            pltpu.VMEM((plane - 1, 2 * slots, 128), f32),
            pltpu.VMEM((plane, steps, width), bf16),
            pltpu.VMEM((plane - 1, steps, width), bf16),
            pltpu.VMEM((plane, ring, steps, width), bf16),
            pltpu.VMEM((2, all_rows // 2, w_down.shape[0]), bf16),
            pltpu.VMEM((all_rows // 2, width), bf16),
            pltpu.VMEM((all_rows // 2, width), bf16),
            pltpu.VMEM((chips, ring, steps, width), bf16),
            pltpu.VMEM((chips - 1, ring, steps, width), bf16),
            pltpu.VMEM((ring - 1, steps, width), bf16),
            pltpu.VMEM((ring - 1, steps, width), bf16),
            pltpu.VMEM((plane, steps, width), bf16),
            pltpu.SemaphoreType.DMA((7,)),
            pltpu.SemaphoreType.DMA((2, slots)),
            pltpu.SemaphoreType.DMA((copies,)),
            pltpu.SemaphoreType.DMA((copies,)),
        ],
        compiler_params=pltpu.CompilerParams(collective_id=0, has_side_effects=True),
    )(*scalars, *vectors, *matrices)


def whole_layer(
    tokens,
    slot_of,
    cache_len,
    owner_shard,
    cache_keys,
    stored_values,
    attn_gain,
    w_query,
    key_matrix,
    value_matrix,
    query_gain,
    key_norm_weight,
    w_out,
    mlp_gain,
    w_gate,
    w_up,
    w_down,
):
    plane, ring = lax.axis_size("seq"), lax.axis_size("req")
    slots, steps = owner_shard.shape
    head_dim = query_gain.shape[0]
    half = head_dim // 2
    position = (cache_len[:, None] + jnp.arange(steps, dtype=jnp.int32)).astype(jnp.float32)
    frequency = ROPE_BASE ** (-2.0 * jnp.arange(half, dtype=jnp.float32) / head_dim)
    angles = position.reshape(-1, 1) * frequency
    cosine, sine = jnp.cos(angles), jnp.sin(angles)
    outputs, incoming = run_layer(
        (slot_of, cache_len, owner_shard.T),
        (
            tokens,
            attn_gain.reshape(-1, 128),
            query_gain.reshape(1, -1),
            key_norm_weight.reshape(1, -1),
            jnp.concatenate([cosine, cosine], axis=1),
            jnp.concatenate([-sine, sine], axis=1),
            mlp_gain.reshape(-1, 128),
        ),
        (
            w_query, key_matrix, value_matrix, cache_keys, stored_values, w_out,
            w_gate.T, w_up.T, w_down,
        ),
        ring, plane, steps,
    )
    owned_here = owner_shard == lax.axis_index("seq")
    appended = jnp.where(owned_here[..., None], incoming, jnp.zeros((), jnp.bfloat16))
    return (outputs.astype(jnp.bfloat16), appended[:, None])


def body(
    tokens,
    slot_of,
    cache_len,
    owner_shard,
    cache_keys,
    stored_values,
    attn_gain,
    w_query,
    key_matrix,
    value_matrix,
    query_gain,
    key_norm_weight,
    w_out,
    mlp_gain,
    w_gate,
    w_up,
    w_down,
):
    group_id = lax.axis_index("req")
    shard_id = lax.axis_index("seq")
    shard_count = lax.axis_size("seq")
    row_count = cache_len.shape[0]
    span_len = cache_keys.shape[1]
    step_count, model_width = tokens.shape[1:]
    head_dim = query_gain.shape[0]
    kv_heads = cache_keys.shape[2] // head_dim
    query_heads = w_query.shape[1] * shard_count // head_dim
    heads_here = query_heads // shard_count
    all_rows = row_count * step_count
    arrived = lax.all_gather(tokens, "req", axis=0, tiled=True)
    slot_ids = group_id * row_count + jnp.arange(row_count, dtype=jnp.int32)
    selector = (slot_of[None, :] == slot_ids[:, None]).astype(jnp.bfloat16)
    inputs = jnp.einsum("ji,isd->jsd", selector, arrived, preferred_element_type=jnp.float32)
    current = inputs.reshape(all_rows, model_width)
    normed = root_mean_scale(current, attn_gain).astype(jnp.bfloat16)
    parts = [
        jnp.dot(normed, matrix, preferred_element_type=jnp.float32).astype(jnp.bfloat16)
        for matrix in (w_query, key_matrix, value_matrix)
    ]
    cut = [parts[0].shape[1], parts[0].shape[1] + parts[1].shape[1]]
    gathered = lax.all_gather(jnp.concatenate(parts, axis=1), "seq", axis=0)
    gathered = jnp.transpose(gathered, (1, 0, 2))
    query_raw = gathered[:, :, :cut[0]].reshape(row_count, step_count, query_heads, head_dim)
    key_raw = gathered[:, :, cut[0]:cut[1]].reshape(row_count, step_count, kv_heads, head_dim)
    incoming_values = gathered[:, :, cut[1]:].reshape(row_count, step_count, kv_heads * head_dim)
    position = (cache_len[:, None] + jnp.arange(step_count, dtype=jnp.int32)).astype(jnp.float32)
    queries = apply_rotary(
        root_mean_scale(query_raw.astype(jnp.float32), query_gain), position[..., None]
    ).astype(jnp.bfloat16)
    incoming_keys = apply_rotary(
        root_mean_scale(key_raw.astype(jnp.float32), key_norm_weight), position[..., None]
    ).astype(jnp.bfloat16).reshape(row_count, step_count, kv_heads * head_dim)
    owned_here = owner_shard == shard_id
    pad = 128
    widen = ((0, 0), (0, pad - step_count), (0, 0))
    live = jnp.pad(owned_here.astype(jnp.int32), ((0, 0), (0, pad - step_count)))
    live = jnp.broadcast_to(live[:, None, :], (row_count, 8, pad))
    here = cache_len - shard_id * span_len
    packed_rows = step_count * query_heads
    wide_dim = kv_heads * head_dim
    slot_block = lambda *shape: pl.BlockSpec((1,) + shape, lambda i, *_: (i,) + (0,) * len(shape))
    out_type = jax.ShapeDtypeStruct((row_count, packed_rows, head_dim), jnp.float32)
    block_out, block_max, block_sum = pl.pallas_call(
        functools.partial(attention_kernel, kv_heads, query_heads),
        out_shape=(out_type,) * 3,
        grid_spec=pltpu.PrefetchScalarGridSpec(
            num_scalar_prefetch=1,
            grid=(row_count,),
            in_specs=[
                slot_block(8, pad),
                slot_block(packed_rows, head_dim),
                slot_block(span_len, wide_dim),
                slot_block(span_len, wide_dim),
                slot_block(pad, wide_dim),
                slot_block(pad, wide_dim),
            ],
            out_specs=[slot_block(packed_rows, head_dim)] * 3,
        ),
    )(
        here,
        live,
        queries.reshape(row_count, packed_rows, head_dim),
        cache_keys,
        stored_values,
        jnp.pad(incoming_keys, widen),
        jnp.pad(incoming_values, widen),
    )
    split = lambda a: a.reshape(all_rows, shard_count, heads_here, -1)
    stats = jnp.concatenate([split(block_max)[..., :1], split(block_sum)[..., :1]], axis=-1)
    payload = jnp.concatenate(
        [
            split(block_out).reshape(all_rows, shard_count, -1),
            stats.reshape(all_rows, shard_count, -1),
        ],
        axis=-1,
    )
    traded = lax.all_to_all(payload, "seq", split_axis=1, concat_axis=0, tiled=False)
    wide_out = heads_here * head_dim
    outs = traded[..., :wide_out].reshape(shard_count, all_rows, heads_here, head_dim)
    stats = traded[..., wide_out:].reshape(shard_count, all_rows, heads_here, 2)
    top = jnp.max(stats[..., 0], axis=0)
    factor = jnp.exp(stats[..., 0] - top)
    numer = jnp.sum(factor[..., None] * outs, axis=0)
    denom = jnp.sum(factor * stats[..., 1], axis=0)
    attended = (numer / denom[..., None]).astype(jnp.bfloat16).reshape(all_rows, wide_out)
    projected = lax.psum_scatter(
        jnp.dot(attended, w_out, preferred_element_type=jnp.float32),
        "seq",
        scatter_dimension=0,
        tiled=True,
    )
    rows_here = all_rows // shard_count
    residual = projected + lax.dynamic_slice_in_dim(current, shard_id * rows_here, rows_here, 0)
    mlp_in = root_mean_scale(residual, mlp_gain).astype(jnp.bfloat16)
    piece = lax.all_gather(mlp_in, ("req", "seq"), axis=0, tiled=True)
    gate_part = jnp.dot(piece, w_gate, preferred_element_type=jnp.float32)
    up_part = jnp.dot(piece, w_up, preferred_element_type=jnp.float32)
    hidden = (jax.nn.silu(gate_part) * up_part).astype(jnp.bfloat16)
    down = lax.psum_scatter(
        jnp.dot(hidden, w_down, preferred_element_type=jnp.float32),
        ("req", "seq"),
        scatter_dimension=0,
        tiled=True,
    )
    finished = (residual + down).astype(jnp.bfloat16)
    outputs = lax.all_gather(finished, "seq", axis=0, tiled=True)
    outputs = outputs.reshape(row_count, step_count, model_width)
    stacked_incoming = jnp.concatenate([incoming_keys, incoming_values], axis=-1)
    appended = jnp.where(owned_here[..., None], stacked_incoming, jnp.zeros((), jnp.bfloat16))
    return (outputs, appended[:, None])


def solution(mesh):
    in_specs = (
        P("req", None, None),
        P(),
        P("req"),
        P("req", None),
        P("req", "seq", None),
        P("req", "seq", None),
        P(),
        P(None, "seq"),
        P(None, "seq"),
        P(None, "seq"),
        P(),
        P(),
        P("seq", None),
        P(),
        P(None, ("req", "seq")),
        P(None, ("req", "seq")),
        P(("req", "seq"), None),
    )
    out_specs = (P("req", None, None), P("req", "seq", None, None))

    def layer(*arrays):
        kv_heads = arrays[4].shape[2] // arrays[10].shape[0]
        row_count = arrays[2].shape[0]
        shards = lax.axis_size("seq")
        if row_count == shards and kv_heads == shards and shards % 2 == 0:
            return whole_layer(*arrays)
        return body(*arrays)

    return jax.shard_map(layer, mesh=mesh, in_specs=in_specs, out_specs=out_specs, check_vma=False)
```

```python
import functools
import math

import jax
import jax.numpy as jnp
from jax import lax
from jax.experimental import pallas as pl
from jax.experimental.pallas import tpu as pltpu
from jax.sharding import PartitionSpec as P

EPSILON = 1e-06
ROPE_BASE = 1000000.0
MASKED = -1e30


def root_mean_scale(tensor, gain_vec):
    mean_square = jnp.mean(tensor * tensor, axis=-1, keepdims=True)
    return tensor * lax.rsqrt(mean_square + EPSILON) * gain_vec


def apply_rotary(tensor, positions):
    half_dim = tensor.shape[-1] // 2
    frequency = ROPE_BASE ** (-2.0 * jnp.arange(half_dim, dtype=jnp.float32) / tensor.shape[-1])
    angles = positions[..., None] * frequency
    cosine = jnp.cos(angles)
    sine_part = jnp.sin(angles)
    front_half = tensor[..., :half_dim]
    back_half = tensor[..., half_dim:]
    return jnp.concatenate(
        [front_half * cosine - back_half * sine_part, back_half * cosine + front_half * sine_part],
        axis=-1,
    )


def attention_kernel(kv_heads, query_heads, here_ref, live_ref, q_ref, k_ref, v_ref, fk_ref, fv_ref,
                     out_ref, max_ref, sum_ref):
    slot = pl.program_id(0)
    rows, head_dim = q_ref.shape[1], q_ref.shape[2]
    span = k_ref.shape[1]
    pad = fk_ref.shape[1]
    width = kv_heads * head_dim
    group = query_heads // kv_heads
    scale = 1.0 / math.sqrt(head_dim)
    own_kv = lax.rem(lax.broadcasted_iota(jnp.int32, (rows, width), 0), query_heads) // group
    lane_kv = lax.broadcasted_iota(jnp.int32, (rows, width), 1) // head_dim
    q = q_ref[0]
    wide = jnp.where(own_kv == lane_kv, jnp.concatenate([q] * kv_heads, axis=1), jnp.zeros((), q.dtype))
    nt = (((1,), (1,)), ((), ()))
    scores = lax.dot_general(wide, k_ref[0], nt, preferred_element_type=jnp.float32) * scale
    in_cache = lax.broadcasted_iota(jnp.int32, (rows, span), 1) < here_ref[slot]
    scores = jnp.where(in_cache, scores, MASKED)
    fresh = lax.dot_general(wide, fk_ref[0], nt, preferred_element_type=jnp.float32) * scale
    step_row = lax.broadcasted_iota(jnp.int32, (rows, pad), 0) // query_heads
    step_lane = lax.broadcasted_iota(jnp.int32, (rows, pad), 1)
    live = (step_lane <= step_row) & (live_ref[0, 0:1, :] > 0)
    fresh = jnp.where(live, fresh, MASKED)
    top = jnp.maximum(
        jnp.max(scores, axis=1, keepdims=True), jnp.max(fresh, axis=1, keepdims=True)
    )
    weights = jnp.where(in_cache, jnp.exp(scores - top), 0.0)
    fresh_weights = jnp.where(live, jnp.exp(fresh - top), 0.0)
    total = jnp.sum(weights, axis=1, keepdims=True) + jnp.sum(fresh_weights, axis=1, keepdims=True)
    product = jnp.dot(weights.astype(jnp.bfloat16), v_ref[0], preferred_element_type=jnp.float32)
    product = product + jnp.dot(
        fresh_weights.astype(jnp.bfloat16), fv_ref[0], preferred_element_type=jnp.float32
    )
    product = jnp.where(own_kv == lane_kv, product, 0.0)
    picked = product[:, :head_dim]
    for head in range(1, kv_heads):
        picked = picked + product[:, head * head_dim:(head + 1) * head_dim]
    out_ref[0] = picked
    max_ref[0] = jnp.broadcast_to(top, (rows, head_dim))
    sum_ref[0] = jnp.broadcast_to(total, (rows, head_dim))


def unfolded(folded_ref):
    folded = folded_ref[...]
    return jnp.concatenate([folded[i:i + 1] for i in range(folded.shape[0])], axis=1)


def layer_kernel(ring, plane, steps, slot_ref, length_ref, owner_ref, tokens_ref, attn_gain_ref, query_gain_ref,
                 key_gain_ref, cosine_ref, sine_ref, gain_ref, query_hbm, key_hbm, value_hbm, keys_hbm, stored_hbm,
                 w_out_hbm, gate_hbm, up_hbm, down_hbm, out_ref, incoming_ref, w_query, w_key, w_value, keys, stored,
                 w_out, w_gate, w_up, w_down, raw_send, raw_land, token_send, token_land, fresh, part_send,
                 part_land, stat_send, stat_land, proj_send, proj_land, mlp_all, hidden_ref,
                 half_send, half_land, quad_send, quad_land, ring_send, ring_land, final, weight_sem, cache_sem, send_sem,
                 recv_sem):
    group = lax.axis_index("req")
    shard = lax.axis_index("seq")
    chips = plane // 2
    core, chip = lax.rem(shard, 2), shard // 2
    other = 1 - core
    partner = chip * 2 + other
    order = core * chips + chip
    mesh_type = pl.DeviceIdType.MESH
    bf16, f32 = jnp.bfloat16, jnp.float32
    nt = (((1,), (1,)), ((), ()))
    iota = lambda shape, axis: lax.broadcasted_iota(jnp.int32, shape, axis)

    plane_peers = [lax.rem(shard + d, plane) for d in range(1, plane)]
    ring_peers = [lax.rem(group + d, ring) for d in range(1, ring)]
    chip_peers = [lax.rem(chip + d, chips) * 2 + core for d in range(1, chips)]
    barrier = pltpu.get_barrier_semaphore()
    for peer in plane_peers:
        pl.semaphore_signal(barrier, inc=1, device_id=(group, peer), device_id_type=mesh_type)
    for peer in ring_peers:
        pl.semaphore_signal(barrier, inc=1, device_id=(peer, shard), device_id_type=mesh_type)
    loads = [
        pltpu.make_async_copy(src, dst, weight_sem.at[i])
        for i, (src, dst) in enumerate(
            (
                (query_hbm, w_query), (key_hbm, w_key), (value_hbm, w_value),
                (w_out_hbm, w_out), (gate_hbm, w_gate), (up_hbm, w_up), (down_hbm, w_down),
            )
        )
    ]
    slots = keys.shape[0]
    cached = [
        (
            pltpu.make_async_copy(keys_hbm.at[j], keys.at[j], cache_sem.at[0, j]),
            pltpu.make_async_copy(stored_hbm.at[j], stored.at[j], cache_sem.at[1, j]),
        )
        for j in range(slots)
    ]
    for copy in loads[:3]:
        copy.start()
    for pair in cached:
        pair[0].start()
        pair[1].start()
    for copy in loads[3:]:
        copy.start()
    weights = loads[3:]
    used = [0]
    sent = []

    def send(src, dst, device):
        index = used[0]
        used[0] += 1
        copy = pltpu.make_async_remote_copy(
            src_ref=src, dst_ref=dst, send_sem=send_sem.at[index], recv_sem=recv_sem.at[index],
            device_id=device, device_id_type=mesh_type,
        )
        copy.start()
        sent.append(copy)
        return copy

    local, _, width = tokens_ref.shape
    head_dim = query_gain_ref.shape[1]
    rows = slots * steps
    group_size = w_query.shape[1] // head_dim
    flat = tokens_ref[...].astype(f32).reshape(local * steps, width)
    normed = root_mean_scale(flat, unfolded(attn_gain_ref)).astype(bf16)
    flat = flat.astype(bf16)
    tall, short = ring * rows, ring * steps
    slot_row, slot_lane = iota((tall, local * steps), 0), iota((tall, local * steps), 1)
    own_row, own_lane = iota((short, local * steps), 0), iota((short, local * steps), 1)
    pick = jnp.zeros((tall, local * steps), f32)
    pick_own = jnp.zeros((short, local * steps), f32)
    for i in range(local):
        slot = slot_ref[group * local + i]
        pick = jnp.where((slot_lane // steps == i) & (slot_row // steps == slot), 1.0, pick)
        pick_own = jnp.where(
            (own_lane // steps == i) & (own_row // steps * slots + shard == slot), 1.0, pick_own
        )
    pick = jnp.where(slot_row % steps == slot_lane % steps, pick, 0.0).astype(bf16)
    pick_own = jnp.where(own_row % steps == own_lane % steps, pick_own, 0.0).astype(bf16)
    raw = []
    for copy, matrix in zip(loads[:3], (w_query, w_key, w_value)):
        copy.wait()
        raw.append(jnp.dot(normed, matrix[...], preferred_element_type=f32).astype(bf16))
    raw = jnp.dot(pick, jnp.concatenate(raw, axis=1), preferred_element_type=f32).astype(bf16)
    for target in range(ring):
        raw_send[target] = raw[target * rows:(target + 1) * rows]
    pl.semaphore_wait(barrier, plane - 1 + ring - 1)
    copies = [send(raw_send.at[peer], raw_land.at[d], (peer, shard)) for d, peer in enumerate(ring_peers)]
    chosen = jnp.dot(pick_own, flat, preferred_element_type=f32)
    for target in range(ring):
        token_send[target] = chosen[target * steps:(target + 1) * steps].astype(bf16)
    raw = raw_send[group].astype(f32)
    for d, copy in enumerate(copies):
        copy.wait_recv()
        raw = raw + raw_land[d].astype(f32)
    token_copies = [
        send(token_send.at[peer], token_land.at[d], (peer, shard)) for d, peer in enumerate(ring_peers)
    ]
    cosine, sine = cosine_ref[...], sine_ref[...]

    def turned(tensor, gain_vec):
        scaled = root_mean_scale(tensor, gain_vec)
        return scaled * cosine + pltpu.roll(scaled, head_dim // 2, 1) * sine

    heads = [turned(raw[:, g * head_dim:(g + 1) * head_dim], query_gain_ref[...]) for g in range(group_size)]
    packed = rows * group_size
    by_head = jnp.concatenate(heads, axis=0).astype(bf16)
    row, lane = iota((packed, packed), 0), iota((packed, packed), 1)
    swap = jnp.where(lane == row % group_size * rows + row // group_size, 1.0, 0.0).astype(bf16)
    back = jnp.where(lane == row % rows * group_size + row // rows, 1.0, 0.0).astype(bf16)
    fresh[order, :packed] = jnp.dot(swap, by_head, preferred_element_type=f32).astype(bf16)
    key_at, value_at = packed, packed + rows
    wide = group_size * head_dim
    fresh[order, key_at:value_at] = turned(raw[:, wide:wide + head_dim], key_gain_ref[...]).astype(bf16)
    fresh[order, value_at:] = raw[:, wide + head_dim:].astype(bf16)
    own = fresh.at[order]
    copies = [send(own, own, (group, peer)) for peer in chip_peers]
    across = [send(own, own, (group, partner))]
    for d, copy in enumerate(copies):
        copy.wait_recv()
        came = fresh.at[core * chips + lax.rem(chip + chips - (d + 1), chips)]
        across.append(send(came, came, (group, partner)))
    for copy in across:
        copy.wait_recv()

    place = [(k % 2) * chips + k // 2 for k in range(plane)]
    new_keys = jnp.concatenate([fresh[p, key_at:value_at] for p in place], axis=1)
    new_values = jnp.concatenate([fresh[p, value_at:] for p in place], axis=1)
    span = keys.shape[1]
    block = steps * group_size
    scale = 1.0 / math.sqrt(head_dim)
    all_queries = plane * block
    position = iota((all_queries, span), 1)
    step_row = iota((all_queries, rows), 0) % block // group_size
    fresh_lane = iota((all_queries, rows), 1)
    stat_lane = iota((all_queries, 128), 1)
    stats = jnp.zeros((all_queries, 128), f32)
    empty = jnp.zeros((block, head_dim), bf16)
    pair_dim = 2 * head_dim
    halves = 4
    part_copies = []
    for j in range(slots):
        cached[j][0].wait()
        pieces, new_pieces = [], []
        for k in range(0, plane, 2):
            first = fresh[place[k], j * block:(j + 1) * block]
            second = fresh[place[k + 1], j * block:(j + 1) * block]
            both = jnp.concatenate(
                [jnp.concatenate([first, empty], axis=1), jnp.concatenate([empty, second], axis=1)], axis=0
            )
            lanes = slice(k * head_dim, k * head_dim + pair_dim)
            pieces.append(lax.dot_general(both, keys[j, :, lanes], nt, preferred_element_type=f32))
            new_pieces.append(lax.dot_general(both, new_keys[:, lanes], nt, preferred_element_type=f32))
        in_cache = position < length_ref[j] - shard * span
        scores = jnp.where(in_cache, jnp.concatenate(pieces, axis=0) * scale, MASKED)
        live = fresh_lane < 0
        for t in range(steps):
            target = jnp.where(owner_ref[t, j] == shard, j * steps + t, -1)
            live = live | ((fresh_lane == target) & (step_row >= t))
        new_scores = jnp.where(live, jnp.concatenate(new_pieces, axis=0) * scale, MASKED)
        top = jnp.maximum(
            jnp.max(scores, axis=1, keepdims=True), jnp.max(new_scores, axis=1, keepdims=True)
        )
        portions = jnp.where(in_cache, jnp.exp(scores - top), 0.0)
        new_portions = jnp.where(live, jnp.exp(new_scores - top), 0.0)
        total = jnp.sum(portions, axis=1, keepdims=True) + jnp.sum(new_portions, axis=1, keepdims=True)
        portions, new_portions = portions.astype(bf16), new_portions.astype(bf16)
        stats = jnp.where(stat_lane == j, top, jnp.where(stat_lane == slots + j, total, stats))
        cached[j][1].wait()
        for k in range(0, plane, 2):
            lanes = slice(k * head_dim, k * head_dim + pair_dim)
            span_rows = slice(k * block, (k + 2) * block)
            product = jnp.dot(portions[span_rows], stored[j, :, lanes], preferred_element_type=f32)
            product = product + jnp.dot(
                new_portions[span_rows], new_values[:, lanes], preferred_element_type=f32
            )
            at = slice(j * block, (j + 1) * block)
            part_send[k, at] = product[:block, :head_dim].astype(bf16)
            part_send[k + 1, at] = product[block:, head_dim:].astype(bf16)
        if (j + 1) % (slots // halves) == 0:
            cut = pl.ds((j + 1 - slots // halves) * block, slots // halves * block)
            for d, peer in enumerate(plane_peers):
                part_copies.append(
                    send(part_send.at[peer, cut], part_land.at[d, cut], (group, peer))
                )
    stat_send[...] = jnp.transpose(stats)[:2 * slots]
    stat_copies = [send(stat_send, stat_land.at[d], (group, peer)) for d, peer in enumerate(plane_peers)]
    for copy in stat_copies:
        copy.wait_recv()
    tops = [stat_send[:slots]] + [stat_land[d, :slots] for d in range(plane - 1)]
    sums = [stat_send[slots:]] + [stat_land[d, slots:] for d in range(plane - 1)]
    joint = functools.reduce(jnp.maximum, tops)
    factors = [jnp.exp(value - joint) for value in tops]
    denom = functools.reduce(jnp.add, [f * s for f, s in zip(factors, sums)])
    here = iota((packed, 128), 1) == iota((packed, 128), 0) % block + shard * block
    columns = []
    for factor in factors:
        spread = jnp.broadcast_to((factor / denom)[:, None, :], (slots, block, 128)).reshape(packed, 128)
        columns.append(jnp.sum(jnp.where(here, spread, 0.0), axis=1, keepdims=True))
    for copy in part_copies:
        copy.wait_recv()
    blended = columns[0] * part_send[shard].astype(f32)
    for d in range(plane - 1):
        blended = blended + columns[d + 1] * part_land[d].astype(f32)
    blended = jnp.dot(back, blended.astype(bf16), preferred_element_type=f32).astype(bf16)
    attended = jnp.concatenate([blended[g * rows:(g + 1) * rows] for g in range(group_size)], axis=1)
    current = token_send[group].astype(f32)
    for d, copy in enumerate(token_copies):
        copy.wait_recv()
        current = current + token_land[d].astype(f32)

    weights[0].wait()
    projected = jnp.dot(attended, w_out[...], preferred_element_type=jnp.float32)
    for target in range(plane):
        proj_send[target] = projected[target * steps:(target + 1) * steps].astype(jnp.bfloat16)
    copies = [
        send(proj_send.at[peer], proj_land.at[d], (group, peer))
        for d, peer in enumerate(plane_peers)
    ]
    for at, fresh_rows in ((0, new_keys), (plane * head_dim, new_values)):
        fresh_rows = fresh_rows.astype(f32)
        for j in range(slots):
            incoming_ref[j, :, at:at + plane * head_dim] = fresh_rows[j * steps:(j + 1) * steps].astype(bf16)
    residual = current + proj_send[shard].astype(jnp.float32)
    for d, copy in enumerate(copies):
        copy.wait_recv()
        residual = residual + proj_land[d].astype(jnp.float32)
    mlp_all[order, group] = root_mean_scale(residual, unfolded(gain_ref)).astype(jnp.bfloat16)

    own = mlp_all.at[order, group]
    ring_copies = [None] + [send(own, own, (peer, shard)) for peer in ring_peers]
    spread_copies, across = [], []
    for d, copy in enumerate(ring_copies):
        source = lax.rem(group + ring - d, ring)
        if copy is not None:
            copy.wait_recv()
        held = mlp_all.at[order, source]
        spread_copies.append([send(held, held, (group, peer)) for peer in chip_peers])
        across.append(send(held, held, (group, partner)))
    for d, copies in enumerate(spread_copies):
        source = lax.rem(group + ring - d, ring)
        for e, copy in enumerate(copies):
            copy.wait_recv()
            held = mlp_all.at[core * chips + lax.rem(chip + chips - (e + 1), chips), source]
            across.append(send(held, held, (group, partner)))
    for copy in across:
        copy.wait_recv()

    width = mlp_all.shape[-1]
    rows = plane * ring * steps
    mlp_in = mlp_all[...].astype(jnp.float32).reshape(rows, width).astype(jnp.bfloat16)
    weights[1].wait()
    gate_part = lax.dot_general(mlp_in, w_gate[...], nt, preferred_element_type=jnp.float32)
    weights[2].wait()
    up_part = lax.dot_general(mlp_in, w_up[...], nt, preferred_element_type=jnp.float32)
    hidden = (gate_part / (1.0 + jnp.exp(-gate_part)) * up_part).astype(jnp.bfloat16)
    weights[3].wait()
    half = rows // 2
    hidden_ref[0] = hidden[:half]
    hidden_ref[1] = hidden[half:]
    half_send[...] = jnp.dot(hidden_ref[other], w_down[...], preferred_element_type=jnp.float32).astype(
        jnp.bfloat16
    )
    copy = send(half_send, half_land, (group, partner))
    both = jnp.dot(hidden_ref[core], w_down[...], preferred_element_type=jnp.float32)
    copy.wait_recv()
    both = both + half_land[...].astype(jnp.float32)
    for target in range(chips * ring):
        quad_send[target // ring, target % ring] = both[target * steps:(target + 1) * steps].astype(
            jnp.bfloat16
        )
    targets = ring_peers + [group]
    quad_copies = [
        [
            send(quad_send.at[peer // 2, target], quad_land.at[e, target], (group, peer))
            for e, peer in enumerate(chip_peers)
        ]
        for target in targets
    ]
    ring_copies = []
    for d, target in enumerate(targets):
        summed = quad_send[chip, target].astype(jnp.float32)
        for e, copy in enumerate(quad_copies[d]):
            copy.wait_recv()
            summed = summed + quad_land[e, target].astype(jnp.float32)
        if d < ring - 1:
            ring_send[d] = summed.astype(jnp.bfloat16)
            ring_copies.append(send(ring_send.at[d], ring_land.at[d], (target, shard)))
    total = residual + summed
    for d, copy in enumerate(ring_copies):
        copy.wait_recv()
        total = total + ring_land[d].astype(jnp.float32)
    final[shard] = total.astype(jnp.bfloat16)
    own = final.at[shard]
    copies = [send(own, own, (group, peer)) for peer in plane_peers]
    for copy in copies:
        copy.wait_recv()
    out_ref[...] = final[...]
    for copy in sent:
        copy.wait_send()


def run_layer(scalars, vectors, matrices, ring, plane, steps):
    tokens = vectors[0]
    w_query, key_matrix, value_matrix, cache_keys, stored_values, w_out, w_gate, w_up, w_down = matrices
    width = w_out.shape[1]
    head_dim = key_matrix.shape[1]
    slots = cache_keys.shape[0]
    all_rows = plane * ring * steps
    rows = slots * steps
    packed = rows * (w_query.shape[1] // head_dim)
    made = w_query.shape[1] + 2 * head_dim
    chips = plane // 2
    bf16, f32 = jnp.bfloat16, jnp.float32
    copies = 7 * (plane - 1) + 4 * (ring - 1) + 2 * chips + ring * (3 * chips - 1) + 2
    vmem = pl.BlockSpec(memory_space=pltpu.VMEM)
    smem = pl.BlockSpec(memory_space=pltpu.SMEM)
    anywhere = pl.BlockSpec(memory_space=pl.ANY)
    return pl.pallas_call(
        functools.partial(layer_kernel, ring, plane, steps),
        out_shape=(
            jax.ShapeDtypeStruct((plane, steps, width), bf16),
            jax.ShapeDtypeStruct((slots, steps, 2 * plane * head_dim), bf16),
        ),
        in_specs=[smem] * len(scalars) + [vmem] * len(vectors) + [anywhere] * len(matrices),
        out_specs=(vmem, vmem),
        scratch_shapes=[pltpu.VMEM(matrix.shape, bf16) for matrix in matrices] + [
            pltpu.VMEM((ring, rows, made), bf16),
            pltpu.VMEM((ring - 1, rows, made), bf16),
            pltpu.VMEM((ring, steps, width), bf16),
            pltpu.VMEM((ring - 1, steps, width), bf16),
            pltpu.VMEM((plane, packed + 2 * rows, head_dim), bf16),
            pltpu.VMEM((plane, packed, head_dim), bf16),
            pltpu.VMEM((plane - 1, packed, head_dim), bf16),
            pltpu.VMEM((2 * slots, 128), f32),
            pltpu.VMEM((plane - 1, 2 * slots, 128), f32),
            pltpu.VMEM((plane, steps, width), bf16),
            pltpu.VMEM((plane - 1, steps, width), bf16),
            pltpu.VMEM((plane, ring, steps, width), bf16),
            pltpu.VMEM((2, all_rows // 2, w_down.shape[0]), bf16),
            pltpu.VMEM((all_rows // 2, width), bf16),
            pltpu.VMEM((all_rows // 2, width), bf16),
            pltpu.VMEM((chips, ring, steps, width), bf16),
            pltpu.VMEM((chips - 1, ring, steps, width), bf16),
            pltpu.VMEM((ring - 1, steps, width), bf16),
            pltpu.VMEM((ring - 1, steps, width), bf16),
            pltpu.VMEM((plane, steps, width), bf16),
            pltpu.SemaphoreType.DMA((7,)),
            pltpu.SemaphoreType.DMA((2, slots)),
            pltpu.SemaphoreType.DMA((copies,)),
            pltpu.SemaphoreType.DMA((copies,)),
        ],
        compiler_params=pltpu.CompilerParams(collective_id=0, has_side_effects=True),
    )(*scalars, *vectors, *matrices)


def finish_kernel(shard_ref, owner_ref, final_ref, incoming_ref, out_ref, appended_ref):
    slots, steps, width = incoming_ref.shape
    out_ref[...] = final_ref[...]
    row = lax.broadcasted_iota(jnp.int32, (steps, width), 0)
    for j in range(slots):
        owned = row < 0
        for t in range(steps):
            owned = owned | (row == jnp.where(owner_ref[t, j] == shard_ref[0], t, -1))
        kept = jnp.where(owned, incoming_ref[j].astype(jnp.float32), 0.0)
        appended_ref[j, 0] = kept.astype(appended_ref.dtype)


def run_finish(shard, owner, final, incoming):
    slots, steps, width = incoming.shape
    vmem = pl.BlockSpec(memory_space=pltpu.VMEM)
    smem = pl.BlockSpec(memory_space=pltpu.SMEM)
    return pl.pallas_call(
        finish_kernel,
        out_shape=(
            jax.ShapeDtypeStruct(final.shape, final.dtype),
            jax.ShapeDtypeStruct((slots, 1, steps, width), incoming.dtype),
        ),
        in_specs=[smem, smem, vmem, vmem],
        out_specs=(vmem, vmem),
    )(shard, owner, final, incoming)


def whole_layer(
    tokens,
    slot_of,
    cache_len,
    owner_shard,
    cache_keys,
    stored_values,
    attn_gain,
    w_query,
    key_matrix,
    value_matrix,
    query_gain,
    key_norm_weight,
    w_out,
    mlp_gain,
    w_gate,
    w_up,
    w_down,
):
    plane, ring = lax.axis_size("seq"), lax.axis_size("req")
    slots, steps = owner_shard.shape
    head_dim = query_gain.shape[0]
    half = head_dim // 2
    position = (cache_len[:, None] + jnp.arange(steps, dtype=jnp.int32)).astype(jnp.float32)
    frequency = ROPE_BASE ** (-2.0 * jnp.arange(half, dtype=jnp.float32) / head_dim)
    angles = position.reshape(-1, 1) * frequency
    cosine, sine = jnp.cos(angles), jnp.sin(angles)
    outputs, incoming = run_layer(
        (slot_of, cache_len, owner_shard.T),
        (
            tokens,
            attn_gain.reshape(-1, 128),
            query_gain.reshape(1, -1),
            key_norm_weight.reshape(1, -1),
            jnp.concatenate([cosine, cosine], axis=1),
            jnp.concatenate([-sine, sine], axis=1),
            mlp_gain.reshape(-1, 128),
        ),
        (
            w_query, key_matrix, value_matrix, cache_keys, stored_values, w_out,
            w_gate.T, w_up.T, w_down,
        ),
        ring, plane, steps,
    )
    shard = lax.axis_index("seq").astype(jnp.int32).reshape(1)
    return run_finish(shard, owner_shard.T, outputs, incoming)


def body(
    tokens,
    slot_of,
    cache_len,
    owner_shard,
    cache_keys,
    stored_values,
    attn_gain,
    w_query,
    key_matrix,
    value_matrix,
    query_gain,
    key_norm_weight,
    w_out,
    mlp_gain,
    w_gate,
    w_up,
    w_down,
):
    group_id = lax.axis_index("req")
    shard_id = lax.axis_index("seq")
    shard_count = lax.axis_size("seq")
    row_count = cache_len.shape[0]
    span_len = cache_keys.shape[1]
    step_count, model_width = tokens.shape[1:]
    head_dim = query_gain.shape[0]
    kv_heads = cache_keys.shape[2] // head_dim
    query_heads = w_query.shape[1] * shard_count // head_dim
    heads_here = query_heads // shard_count
    all_rows = row_count * step_count
    arrived = lax.all_gather(tokens, "req", axis=0, tiled=True)
    slot_ids = group_id * row_count + jnp.arange(row_count, dtype=jnp.int32)
    selector = (slot_of[None, :] == slot_ids[:, None]).astype(jnp.bfloat16)
    inputs = jnp.einsum("ji,isd->jsd", selector, arrived, preferred_element_type=jnp.float32)
    current = inputs.reshape(all_rows, model_width)
    normed = root_mean_scale(current, attn_gain).astype(jnp.bfloat16)
    parts = [
        jnp.dot(normed, matrix, preferred_element_type=jnp.float32).astype(jnp.bfloat16)
        for matrix in (w_query, key_matrix, value_matrix)
    ]
    cut = [parts[0].shape[1], parts[0].shape[1] + parts[1].shape[1]]
    gathered = lax.all_gather(jnp.concatenate(parts, axis=1), "seq", axis=0)
    gathered = jnp.transpose(gathered, (1, 0, 2))
    query_raw = gathered[:, :, :cut[0]].reshape(row_count, step_count, query_heads, head_dim)
    key_raw = gathered[:, :, cut[0]:cut[1]].reshape(row_count, step_count, kv_heads, head_dim)
    incoming_values = gathered[:, :, cut[1]:].reshape(row_count, step_count, kv_heads * head_dim)
    position = (cache_len[:, None] + jnp.arange(step_count, dtype=jnp.int32)).astype(jnp.float32)
    queries = apply_rotary(
        root_mean_scale(query_raw.astype(jnp.float32), query_gain), position[..., None]
    ).astype(jnp.bfloat16)
    incoming_keys = apply_rotary(
        root_mean_scale(key_raw.astype(jnp.float32), key_norm_weight), position[..., None]
    ).astype(jnp.bfloat16).reshape(row_count, step_count, kv_heads * head_dim)
    owned_here = owner_shard == shard_id
    pad = 128
    widen = ((0, 0), (0, pad - step_count), (0, 0))
    live = jnp.pad(owned_here.astype(jnp.int32), ((0, 0), (0, pad - step_count)))
    live = jnp.broadcast_to(live[:, None, :], (row_count, 8, pad))
    here = cache_len - shard_id * span_len
    packed_rows = step_count * query_heads
    wide_dim = kv_heads * head_dim
    slot_block = lambda *shape: pl.BlockSpec((1,) + shape, lambda i, *_: (i,) + (0,) * len(shape))
    out_type = jax.ShapeDtypeStruct((row_count, packed_rows, head_dim), jnp.float32)
    block_out, block_max, block_sum = pl.pallas_call(
        functools.partial(attention_kernel, kv_heads, query_heads),
        out_shape=(out_type,) * 3,
        grid_spec=pltpu.PrefetchScalarGridSpec(
            num_scalar_prefetch=1,
            grid=(row_count,),
            in_specs=[
                slot_block(8, pad),
                slot_block(packed_rows, head_dim),
                slot_block(span_len, wide_dim),
                slot_block(span_len, wide_dim),
                slot_block(pad, wide_dim),
                slot_block(pad, wide_dim),
            ],
            out_specs=[slot_block(packed_rows, head_dim)] * 3,
        ),
    )(
        here,
        live,
        queries.reshape(row_count, packed_rows, head_dim),
        cache_keys,
        stored_values,
        jnp.pad(incoming_keys, widen),
        jnp.pad(incoming_values, widen),
    )
    split = lambda a: a.reshape(all_rows, shard_count, heads_here, -1)
    stats = jnp.concatenate([split(block_max)[..., :1], split(block_sum)[..., :1]], axis=-1)
    payload = jnp.concatenate(
        [
            split(block_out).reshape(all_rows, shard_count, -1),
            stats.reshape(all_rows, shard_count, -1),
        ],
        axis=-1,
    )
    traded = lax.all_to_all(payload, "seq", split_axis=1, concat_axis=0, tiled=False)
    wide_out = heads_here * head_dim
    outs = traded[..., :wide_out].reshape(shard_count, all_rows, heads_here, head_dim)
    stats = traded[..., wide_out:].reshape(shard_count, all_rows, heads_here, 2)
    top = jnp.max(stats[..., 0], axis=0)
    factor = jnp.exp(stats[..., 0] - top)
    numer = jnp.sum(factor[..., None] * outs, axis=0)
    denom = jnp.sum(factor * stats[..., 1], axis=0)
    attended = (numer / denom[..., None]).astype(jnp.bfloat16).reshape(all_rows, wide_out)
    projected = lax.psum_scatter(
        jnp.dot(attended, w_out, preferred_element_type=jnp.float32),
        "seq",
        scatter_dimension=0,
        tiled=True,
    )
    rows_here = all_rows // shard_count
    residual = projected + lax.dynamic_slice_in_dim(current, shard_id * rows_here, rows_here, 0)
    mlp_in = root_mean_scale(residual, mlp_gain).astype(jnp.bfloat16)
    piece = lax.all_gather(mlp_in, ("req", "seq"), axis=0, tiled=True)
    gate_part = jnp.dot(piece, w_gate, preferred_element_type=jnp.float32)
    up_part = jnp.dot(piece, w_up, preferred_element_type=jnp.float32)
    hidden = (jax.nn.silu(gate_part) * up_part).astype(jnp.bfloat16)
    down = lax.psum_scatter(
        jnp.dot(hidden, w_down, preferred_element_type=jnp.float32),
        ("req", "seq"),
        scatter_dimension=0,
        tiled=True,
    )
    finished = (residual + down).astype(jnp.bfloat16)
    outputs = lax.all_gather(finished, "seq", axis=0, tiled=True)
    outputs = outputs.reshape(row_count, step_count, model_width)
    stacked_incoming = jnp.concatenate([incoming_keys, incoming_values], axis=-1)
    appended = jnp.where(owned_here[..., None], stacked_incoming, jnp.zeros((), jnp.bfloat16))
    return (outputs, appended[:, None])


def solution(mesh):
    in_specs = (
        P("req", None, None),
        P(),
        P("req"),
        P("req", None),
        P("req", "seq", None),
        P("req", "seq", None),
        P(),
        P(None, "seq"),
        P(None, "seq"),
        P(None, "seq"),
        P(),
        P(),
        P("seq", None),
        P(),
        P(None, ("req", "seq")),
        P(None, ("req", "seq")),
        P(("req", "seq"), None),
    )
    out_specs = (P("req", None, None), P("req", "seq", None, None))

    def layer(*arrays):
        kv_heads = arrays[4].shape[2] // arrays[10].shape[0]
        row_count = arrays[2].shape[0]
        shards = lax.axis_size("seq")
        if row_count == shards and kv_heads == shards and shards % 2 == 0:
            return whole_layer(*arrays)
        return body(*arrays)

    return jax.shard_map(layer, mesh=mesh, in_specs=in_specs, out_specs=out_specs, check_vma=False)
```
